128 devices in a mesh: dp: 4 (over y), row: 8 (over z, core), col: 4 (over x).
Axes of the slice: x: 4, y: 4, z: 4, core: 2. Of those that a mesh axis runs over, the one named last changes fastest.
Arguments:
- gradients: bfloat16 [4, 8192, 14336], P('dp', 'row', 'col'), may hold values from -6 to 6
- test_matrix: int32 [14336, 512], P('col'), may hold values from -3 to 3
- old_basis: float32 [8192, 512], P('row'), may hold values from -0.0625 to 0.0625
- first_moment: float32 [512, 14336], P(('dp', 'row'), 'col'), may hold values from -24 to 24
- second_moment: float32 [512, 14336], P(('dp', 'row'), 'col'), may hold values from 1 to 16
Outputs:
- projected: float32 [512, 14336], P(('dp', 'row'), 'col')
- first_moment_new: float32 [512, 14336], P(('dp', 'row'), 'col')
- second_moment_new: float32 [512, 14336], P(('dp', 'row'), 'col')
The draws below stay inside these ranges and needn't reach their ends.
All inputs are finite; a program needn't handle non-finite values.
Results may differ from the reference program's by a relative error of at most 0.0023.
Values sent between devices are 32-bit elements; how exact they have to be, the bound alone decides.
A program may use at most 128 MiB of HBM per device.

```python
import math
import jax
import jax.numpy as jnp
from jax import lax

M = 8192
N = 14336
R = 512
REPLICAS = 4


def with_ends(drawn, key, least, high):
    longest = drawn.shape.index(max(drawn.shape))
    spots = []
    for shift in (0, 1):
        where = [jax.random.randint(jax.random.fold_in(key, axis), (), 0, length) for axis, length in enumerate(drawn.shape)]
        where[longest] = (where[longest] + shift) % drawn.shape[longest]
        spots.append(tuple(where))
    return drawn.at[spots[0]].set(least).at[spots[1]].set(high)


def steps_of(rng, shape, shards, low, high):
    level = 1.0
    for dim, blocks in shards:
        steps = jax.random.uniform(jax.random.fold_in(jax.random.fold_in(rng, 6), dim), (blocks,), jnp.float32, low / len(shards), high / len(shards))
        level = level * jnp.repeat(jnp.exp(steps), shape[dim] // blocks).reshape((-1,) + (1,) * (len(shape) - 1 - dim))
    return level


def bell_draw(stream_key, dims, spread, limit, split=(), dtype=jnp.bfloat16):
    array = jax.random.normal(stream_key, dims, jnp.float32) * spread
    if len(split) > 0:
        array = steps_of(stream_key, dims, split, -0.22, 0.18) * array
    return jnp.clip(array, min=-limit, max=limit).astype(dtype)


def setup_inputs(seed: int = 0) -> dict:
    arg_keys = jax.random.split(jax.random.key(seed), 6)
    return {
        "gradients": bell_draw(arg_keys[0], (REPLICAS, M, N), 1.0, 6.0, ((0, 4), (1, 8), (2, 4))),
        "test_matrix": with_ends(jax.random.randint(arg_keys[1], (N, R), -3, 4), jax.random.fold_in(arg_keys[1], 1), -3, 3).astype(jnp.int32),
        "old_basis": bell_draw(arg_keys[2], (M, R), M ** -0.5, 0.0625, ((0, 8),), jnp.float32),
        "first_moment": bell_draw(arg_keys[3], (R, N), 4.0, 24.0, ((0, 32), (1, 4)), jnp.float32),
        "second_moment": jnp.clip(jnp.exp(math.log(16.0) - 2.7725887 * jax.random.uniform(arg_keys[4], (R, N), jnp.float32) ** steps_of(arg_keys[4], (R, N), ((0, 32), (1, 4)), -0.2, 0.2)), 1.0, 16.0),
    }


highest = lax.Precision.HIGHEST

def reference(gradients, test_matrix, old_basis, first_moment, second_moment):
    test_values = test_matrix.astype(jnp.bfloat16)
    sketch = jnp.zeros((M, R), jnp.float32)
    for replica in range(REPLICAS):
        sketch = sketch + jnp.dot(gradients[replica].astype(jnp.float32), test_values.astype(jnp.float32), preferred_element_type=jnp.float32)
    gram_total = jnp.dot(sketch.T.astype(jnp.float32), sketch.astype(jnp.float32), precision=highest, preferred_element_type=jnp.float32)
    lower_factor = jnp.linalg.cholesky(gram_total)
    new_basis = jax.scipy.linalg.solve_triangular(lower_factor, sketch.T, lower=True).T
    basis_low = new_basis.astype(jnp.bfloat16)
    projected = jnp.zeros((R, N), jnp.float32)
    for replica in range(REPLICAS):
        projected = projected + jnp.dot(basis_low.T.astype(jnp.float32), gradients[replica].astype(jnp.float32), preferred_element_type=jnp.float32)
    correlation = jnp.dot(new_basis.T.astype(jnp.float32), old_basis.astype(jnp.float32), precision=highest, preferred_element_type=jnp.float32)
    turned_first = jnp.dot(correlation.astype(jnp.float32), first_moment.astype(jnp.float32), precision=highest, preferred_element_type=jnp.float32)
    turned_second = jnp.dot((correlation * correlation).astype(jnp.float32), second_moment.astype(jnp.float32), precision=highest, preferred_element_type=jnp.float32)
    first_new = 0.9 * turned_first + 0.1 * projected
    second_new = 0.95 * turned_second + 0.05 * projected * projected
    return (projected, first_new, second_new)
```

```python
import functools
import jax, jax.numpy as jnp
from jax import lax
from jax.experimental import pallas as pl
from jax.experimental.pallas import tpu as pltpu
from jax.sharding import PartitionSpec as P

HI = lax.Precision.HIGHEST
f32 = jnp.float32


def factor_diag(block, group):
    size = block.shape[0]
    tiles = size // 8
    z = [block[8 * b : 8 * b + 8, :] for b in range(tiles)]
    lane = lax.broadcasted_iota(jnp.int32, (8, size), 1)
    sub = lax.broadcasted_iota(jnp.int32, (8, size), 0)
    full = lambda v: jnp.broadcast_to(v, (8, size))
    for b in range(tiles):
        pivots = jnp.ones((8, size), f32)
        for r in range(0, 8, group):
            j = 8 * b + r
            piv = [[full(z[b][r + t : r + t + 1, j + s : j + s + 1]) for s in range(group)] for t in range(group)]
            inside = (lane >= j) & (lane < j + group)
            rows = [
                jnp.where(inside, (lane == j + t).astype(f32), full(z[b][r + t : r + t + 1, :])) for t in range(group)
            ]
            inv = []
            for t in range(group):
                pivots = jnp.where(sub == r + t, piv[t][t], pivots)
                inv.append(1.0 / piv[t][t])
                for u in range(t + 1, group):
                    m = piv[t][u] * inv[t]
                    for s in range(u, group):
                        piv[u][s] = piv[u][s] - m * piv[t][s]
                    rows[u] = rows[u] - m * rows[t]
            for i in range(b, tiles):
                cols = [full_col(z[i], j + t, size) for t in range(group)]
                acc = jnp.where(inside, (sub - r == lane - j).astype(f32) if i == b else 0.0, z[i])
                for t in range(group):
                    m = cols[t] * inv[t]
                    for u in range(t + 1, group):
                        cols[u] = cols[u] - m * piv[t][u]
                    if i == b:
                        m = jnp.where(sub > r + t, m, 0.0)
                    acc = acc - m * rows[t]
                z[i] = acc
        z[b] = z[b] * lax.rsqrt(pivots)
    out = jnp.concatenate(z, axis=0)
    i = lax.broadcasted_iota(jnp.int32, (size, size), 0)
    k = lax.broadcasted_iota(jnp.int32, (size, size), 1)
    return jnp.where(k <= i, out, 0.0)


def full_col(tile, j, size):
    return jnp.broadcast_to(tile[:, j : j + 1], (8, size))


def inverse_factor(z, group=8, size=128):
    n = z.shape[0]
    blocks = n // size

    def step(k, carry):
        at = pl.ds(pl.multiple_of(k * size, size), size)
        inv = factor_diag(z[at, at], group)
        z[at, :] = jnp.dot(inv, z[at, :], precision=HI, preferred_element_type=f32)
        z[at, at] = inv

        def below(i, c):
            ai = pl.ds(pl.multiple_of(i * size, size), size)
            low = z[at, ai]
            z[ai, at] = jnp.zeros((size, size), f32)
            z[ai, :] = z[ai, :] - lax.dot_general(
                low, z[at, :], (((0,), (0,)), ((), ())), precision=HI, preferred_element_type=f32
            )
            return c

        lax.fori_loop(k + 1, blocks, below, 0)
        return carry

    lax.fori_loop(0, blocks, step, 0)
    row = lax.broadcasted_iota(jnp.int32, (n, n), 0) // size
    col = lax.broadcasted_iota(jnp.int32, (n, n), 1) // size
    z[...] = jnp.where(col <= row, z[...], 0.0)


def chol_kernel(group, a_ref, out_ref):
    out_ref[...] = a_ref[...]
    inverse_factor(out_ref, group)


def inverse_cholesky(gram, group=8, interpret=False):
    n = gram.shape[0]
    return pl.pallas_call(
        functools.partial(chol_kernel, group),
        out_shape=jax.ShapeDtypeStruct((n, n), f32),
        in_specs=[pl.BlockSpec(memory_space=pltpu.VMEM)],
        out_specs=pl.BlockSpec(memory_space=pltpu.VMEM),
        interpret=interpret,
    )(gram)


def local(gradients, test_matrix, old_basis, first_moment, second_moment):
    replica_grad = gradients[0]
    all_first = lax.all_gather(first_moment, ("dp", "row"), axis=0, tiled=True)
    all_second = lax.all_gather(second_moment, ("dp", "row"), axis=0, tiled=True)
    test_values = test_matrix.astype(jnp.bfloat16)
    partial_value = jnp.dot(replica_grad, test_values, preferred_element_type=f32)
    sketch = lax.psum(partial_value, ("dp", "col"))
    both = lax.dot_general(
        sketch,
        jnp.concatenate([sketch, old_basis], axis=1),
        (((0,), (0,)), ((), ())),
        precision=HI,
        preferred_element_type=f32,
    )
    both = lax.psum(both, "row")
    rank = sketch.shape[1]
    inverse = inverse_cholesky(both[:, :rank], 8)
    basis = lax.dot_general(sketch, inverse, (((1,), (1,)), ((), ())), precision=HI, preferred_element_type=f32)
    basis_low = basis.astype(jnp.bfloat16)
    projected = lax.psum_scatter(
        lax.dot_general(basis_low, replica_grad, (((0,), (0,)), ((), ())), preferred_element_type=f32),
        ("dp", "row"),
        scatter_dimension=0,
        tiled=True,
    )
    rank_dev = first_moment.shape[0]
    rank_start = lax.axis_index(("dp", "row")) * rank_dev
    own_inverse = lax.dynamic_slice_in_dim(inverse, rank_start, rank_dev, 0)
    own_rows = jnp.dot(own_inverse, both[:, rank:], precision=HI, preferred_element_type=f32)
    turned_first = jnp.dot(own_rows, all_first, precision=HI, preferred_element_type=f32)
    turned_second = jnp.dot(own_rows * own_rows, all_second, precision=HI, preferred_element_type=f32)
    first_new = 0.9 * turned_first + 0.1 * projected
    second_new = 0.95 * turned_second + 0.05 * projected * projected
    return (projected, first_new, second_new)


def solution(mesh):
    in_specs = (
        P("dp", "row", "col"),
        P("col", None),
        P("row", None),
        P(("dp", "row"), "col"),
        P(("dp", "row"), "col"),
    )
    out_specs = (P(("dp", "row"), "col"), P(("dp", "row"), "col"), P(("dp", "row"), "col"))
    return jax.shard_map(local, mesh=mesh, in_specs=in_specs, out_specs=out_specs, check_vma=False)
```

```python
import functools
import jax, jax.numpy as jnp
from jax import lax
from jax.experimental import pallas as pl
from jax.experimental.pallas import tpu as pltpu
from jax.sharding import PartitionSpec as P

HI = lax.Precision.HIGHEST
f32 = jnp.float32


def factor_diag(block, group):
    size = block.shape[0]
    tiles = size // 8
    z = [block[8 * b : 8 * b + 8, :] for b in range(tiles)]
    lane = lax.broadcasted_iota(jnp.int32, (8, size), 1)
    sub = lax.broadcasted_iota(jnp.int32, (8, size), 0)
    full = lambda v: jnp.broadcast_to(v, (8, size))
    for b in range(tiles):
        pivots = jnp.ones((8, size), f32)
        for r in range(0, 8, group):
            j = 8 * b + r
            piv = [[full(z[b][r + t : r + t + 1, j + s : j + s + 1]) for s in range(group)] for t in range(group)]
            inside = (lane >= j) & (lane < j + group)
            rows = [
                jnp.where(inside, (lane == j + t).astype(f32), full(z[b][r + t : r + t + 1, :])) for t in range(group)
            ]
            inv = []
            for t in range(group):
                pivots = jnp.where(sub == r + t, piv[t][t], pivots)
                inv.append(1.0 / piv[t][t])
                for u in range(t + 1, group):
                    m = piv[t][u] * inv[t]
                    for s in range(u, group):
                        piv[u][s] = piv[u][s] - m * piv[t][s]
                    rows[u] = rows[u] - m * rows[t]
            for i in range(b, tiles):
                cols = [full_col(z[i], j + t, size) for t in range(group)]
                acc = jnp.where(inside, (sub - r == lane - j).astype(f32) if i == b else 0.0, z[i])
                for t in range(group):
                    m = cols[t] * inv[t]
                    for u in range(t + 1, group):
                        cols[u] = cols[u] - m * piv[t][u]
                    if i == b:
                        m = jnp.where(sub > r + t, m, 0.0)
                    acc = acc - m * rows[t]
                z[i] = acc
        z[b] = z[b] * lax.rsqrt(pivots)
    out = jnp.concatenate(z, axis=0)
    i = lax.broadcasted_iota(jnp.int32, (size, size), 0)
    k = lax.broadcasted_iota(jnp.int32, (size, size), 1)
    return jnp.where(k <= i, out, 0.0)


def full_col(tile, j, size):
    return jnp.broadcast_to(tile[:, j : j + 1], (8, size))


def inverse_factor(z, group=8, size=128):
    n = z.shape[0]
    blocks = n // size

    def step(k, carry):
        at = pl.ds(pl.multiple_of(k * size, size), size)
        inv = factor_diag(z[at, at], group)
        z[at, :] = jnp.dot(inv, z[at, :], precision=HI, preferred_element_type=f32)
        z[at, at] = inv

        def below(i, c):
            ai = pl.ds(pl.multiple_of(i * size, size), size)
            low = z[at, ai]
            z[ai, at] = jnp.zeros((size, size), f32)
            z[ai, :] = z[ai, :] - lax.dot_general(
                low, z[at, :], (((0,), (0,)), ((), ())), precision=HI, preferred_element_type=f32
            )
            return c

        lax.fori_loop(k + 1, blocks, below, 0)
        return carry

    lax.fori_loop(0, blocks, step, 0)
    row = lax.broadcasted_iota(jnp.int32, (n, n), 0) // size
    col = lax.broadcasted_iota(jnp.int32, (n, n), 1) // size
    z[...] = jnp.where(col <= row, z[...], 0.0)


MESH = pl.DeviceIdType.MESH
bf16 = jnp.bfloat16
SIDE = 4


def place():
    row = lax.axis_index("row")
    return {"x": lax.axis_index("col"), "y": lax.axis_index("dp"), "z": row // 2, "c": row % 2}


def device(at):
    return (at["y"], at["z"] * 2 + at["c"], at["x"])


def moved(at, axis, step):
    size = 2 if axis == "c" else SIDE
    return {**at, axis: lax.rem(at[axis] + (step % size), size)}


def begin(out):
    out.start()


def sent(out):
    out.wait_send()


def came(out):
    out.wait_recv()


class Links:
    def __init__(self, at, send, recv):
        self.at, self.send, self.recv, self.used, self.started = at, send, recv, 0, []

    def copy(self, src, dst, axis, step):
        i = self.used
        self.used += 1
        out = pltpu.make_async_remote_copy(
            src_ref=src,
            dst_ref=dst,
            send_sem=self.send.at[i],
            recv_sem=self.recv.at[i],
            device_id=device(moved(self.at, axis, step)),
            device_id_type=MESH,
        )
        out.start()
        self.started.append(out)
        return out

    def finish(self):
        for out in self.started:
            out.wait_send()


def greet(at, near, plane):
    barrier = pltpu.get_barrier_semaphore()
    count = 0

    def signal(to):
        pl.semaphore_signal(barrier, inc=1, device_id=device(to), device_id_type=MESH)

    for axis in near:
        for step in range(1, 2 if axis == "c" else SIDE):
            signal(moved(at, axis, step))
            count += 1
    if plane:
        me = at["y"] * 8 + at["z"] * 2 + at["c"]

        def one(step, carry):
            signal({**at, **plane_place(lax.rem(me + step, 32))})
            return carry

        lax.fori_loop(1, 32, one, 0)
        count += 31
    return barrier, count


def plane_place(p):
    return {"y": p // 8, "z": (p // 2) % 4, "c": p % 2}


def tree(own, slots):
    return (own + slots[1]) + (slots[0] + slots[2])


def split3(value):
    high = value.astype(bf16)
    rest = value - high.astype(f32)
    mid = rest.astype(bf16)
    low = (rest - mid.astype(f32)).astype(bf16)
    return high, mid, low


def sketch_kernel(
    tiles, g_hbm, t_hbm, o_hbm, m1_ref, m2_ref, gh_ref, s_ref, mc_ref,
    g_buf, t_buf, t_low, part, half, full, quarter, second, own, o_buf,
    d_buf, core_in, v0, r1, v1, r2, v2, r3, v3, w1, w0,
    send, recv, msend, mrecv, local_sem,
):
    at = place()
    x, y, c = at["x"], at["y"], at["c"]
    me = at["y"] * 8 + at["z"] * 2 + c
    links = Links(at, send, recv)
    barrier, count = greet(at, "x", True)
    first_axis = ("x", "y")

    loads = []

    def load(src, dst):
        out = pltpu.make_async_copy(src, dst, local_sem.at[len(loads)])
        out.start()
        loads.append(out)
        return out

    steps = (2, 1, -1, 0)
    chunks = t_buf.shape[0]
    g_loads, t_loads = {}, {}

    def load_g(i):
        g_loads[i] = [
            load(g_hbm.at[colour, lax.rem(at[first_axis[colour]] + steps[i] % SIDE, SIDE)], g_buf.at[i, colour])
            for colour in range(2)
        ]

    load_g(0)
    for k in range(chunks):
        t_loads[k] = load(t_hbm.at[k], t_buf.at[k])
    for i in (1, 2, 3):
        load_g(i)
    o_loads = [load(o_hbm.at[0, x, y], o_buf.at[0]), load(o_hbm.at[1, y, x], o_buf.at[1])]

    deep = t_buf.shape[1]
    wide = t_buf.shape[2]
    rows = g_buf.shape[2]

    def product(i, k):
        lhs = g_buf[i, :, :, pl.ds(pl.multiple_of(k * deep, deep), deep)].reshape(2 * rows, deep)
        return jnp.dot(lhs, t_low[k], preferred_element_type=f32).reshape(2, rows, wide)

    def matmul(i):
        for out in g_loads[i]:
            out.wait()
        if i == 0:
            for k in range(chunks):
                t_loads[k].wait()
                t_low[k] = t_buf[k].astype(f32).astype(bf16)
                part[i] = product(i, k) + (part[i] if k else 0.0)
        else:
            part[i] = product(i, 0)

            def more(k, carry):
                part[i] += product(i, k)
                return carry

            lax.fori_loop(1, chunks, more, 0)

    def trade(step, moment):
        to = lax.rem(me + step, 32)
        col = pl.ds(pl.multiple_of(lax.rem(to, tiles) * 128, 128), 128)
        return pltpu.make_async_remote_copy(
            src_ref=(m1_ref, m2_ref)[moment].at[:, col],
            dst_ref=mc_ref.at[moment, me],
            send_sem=msend.at[moment, step],
            recv_sem=mrecv.at[moment, step],
            device_id=device({**at, **plane_place(to)}),
            device_id_type=MESH,
        ), to

    def trade_start(step, carry):
        for moment in range(2):
            out, to = trade(step, moment)
            pl.when(to < tiles)(functools.partial(begin, out))
        return carry

    def trade_end(step, carry):
        for moment in range(2):
            out, to = trade(step, moment)
            pl.when(to < tiles)(functools.partial(sent, out))
            pl.when(me < tiles)(functools.partial(came, out))
        return carry

    matmul(0)
    pl.semaphore_wait(barrier, count)
    mid = rows // 2
    up, down = [], []
    for colour, axis in enumerate(first_axis):
        up.append(links.copy(part.at[0, colour, pl.ds(0, mid)], half.at[0, colour], axis, 1))
        down.append(links.copy(part.at[0, colour, pl.ds(mid, mid)], half.at[1, colour], axis, -1))
    matmul(1)
    ups = []
    for colour, axis in enumerate(first_axis):
        up[colour].wait_recv()
        part[1, colour, 0:mid] += half[0, colour]
        ups.append(links.copy(part.at[1, colour], full.at[0, colour], axis, 1))
    matmul(2)
    downs = []
    for colour, axis in enumerate(first_axis):
        down[colour].wait_recv()
        part[2, colour, mid:] += half[1, colour]
        downs.append(links.copy(part.at[2, colour], full.at[1, colour], axis, -1))
    matmul(3)
    later = []
    for colour, axis in enumerate(first_axis):
        other = first_axis[1 - colour]
        ups[colour].wait_recv()
        downs[colour].wait_recv()
        total = part[3, colour] + (full[0, colour] + full[1, colour])
        quarter[colour] = total.reshape(quarter.shape[1:])
        later.append(
            [
                links.copy(
                    quarter.at[colour, lax.rem(at[other] + step, SIDE)], second.at[colour, step - 1], other, step
                )
                for step in (1, 2, 3)
            ]
        )
    for colour in range(2):
        other = first_axis[1 - colour]
        for out in later[colour]:
            out.wait_recv()
        own[colour] = tree(quarter[colour, at[other]], second[colour])

    gather = []
    for colour in range(2):
        other = first_axis[1 - colour]
        here = s_ref.at[colour, at[first_axis[colour]], at[other]]
        s_ref[colour, at[first_axis[colour]], at[other]] = own[colour]
        gather.append([links.copy(own.at[colour], here, other, step) for step in (1, 2, 3)])

    for out in o_loads:
        out.wait()
    mine = own[...].reshape(-1, wide)
    old = o_buf[...].reshape(-1, wide)
    h, m, l = split3(mine)
    left = jnp.concatenate([h, h, m, h, m, l], axis=0)

    def share(value):
        a, b, e = split3(value)
        right = jnp.concatenate([a, b, a, e, b, a], axis=0)
        return lax.dot_general(left, right, (((0,), (0,)), ((), ())), preferred_element_type=f32)

    for kind, value in enumerate((mine, old)):
        for core in range(2):
            out = share(value[:, core * 256 : core * 256 + 256])
            for colour in range(2):
                d_buf[core, colour, kind] = out[:, colour * 128 : colour * 128 + 128].reshape(d_buf.shape[3:])
    across = links.copy(d_buf.at[1 - c], core_in, "c", 1)
    lax.fori_loop(1, 32, trade_start, 0)

    @pl.when(me < tiles)
    def _():
        col = pl.ds(pl.multiple_of(lax.rem(me, tiles) * 128, 128), 128)
        mc_ref[0, me] = m1_ref[:, col]
        mc_ref[1, me] = m2_ref[:, col]

    across.wait_recv()
    v0[...] = d_buf[c] + core_in[...]

    orders = (("x", "y", "z"), ("y", "z", "x"))
    pend = [None, None]

    def scatter(buf, slots, level):
        for colour in range(2):
            axis = orders[colour][level]
            pend[colour] = [
                links.copy(
                    buf.at[colour, :, lax.rem(at[axis] + step, SIDE)], slots.at[colour, step - 1], axis, step
                )
                for step in (1, 2, 3)
            ]

    def waits():
        for colour in range(2):
            for out in pend[colour]:
                out.wait_recv()

    scatter(v0, r1, 0)
    ring = []
    for colour in range(2):
        axis = first_axis[colour]
        for out in gather[colour]:
            out.wait_recv()
        here = s_ref.at[colour, at[axis]]
        ring.append((links.copy(here, here, axis, 1), links.copy(here, here, axis, -1)))
    waits()
    for colour in range(2):
        v1[colour] = tree(v0[colour, :, at[orders[colour][0]]], r1[colour]).reshape(v1.shape[1:])
    scatter(v1, r2, 1)
    waits()
    for colour in range(2):
        v2[colour] = tree(v1[colour, :, at[orders[colour][1]]], r2[colour])
    for colour in range(2):
        axis = orders[colour][2]
        pend[colour] = [links.copy(v2.at[colour], r3.at[colour, step - 1], axis, step) for step in (1, 2, 3)]
    relay = []
    for colour in range(2):
        axis = first_axis[colour]
        ring[colour][0].wait_recv()
        ring[colour][1].wait_recv()
        left_at = lax.rem(at[axis] + 3, SIDE)
        right_at = lax.rem(at[axis] + 1, SIDE)
        lo = s_ref.at[colour, left_at, pl.ds(0, 2)]
        hi = s_ref.at[colour, right_at, pl.ds(2, 2)]
        relay.append((links.copy(lo, lo, axis, 1), links.copy(hi, hi, axis, -1)))
    waits()
    for colour in range(2):
        v3[colour] = tree(v2[colour], r3[colour])
    for colour in range(2):
        axis = orders[colour][1]
        here = w1.at[colour, :, at[axis]]
        w1[colour, :, at[axis]] = v3[colour]
        pend[colour] = [links.copy(v3.at[colour], here, axis, step) for step in (1, 2, 3)]
    waits()
    for colour in range(2):
        axis = orders[colour][0]
        w0[colour, :, at[axis]] = w1[colour]
        pend[colour] = [
            links.copy(w1.at[colour], w0.at[colour, :, at[axis]], axis, step) for step in (1, 2, 3)
        ]
    waits()
    gh_ref[c] = w0[...]
    last = links.copy(w0, gh_ref.at[c], "c", 1)
    last.wait_recv()
    for pair in relay:
        for out in pair:
            out.wait_recv()
    lax.fori_loop(1, 32, trade_end, 0)
    links.finish()


VMEM = pl.BlockSpec(memory_space=pltpu.VMEM)
ANY = pl.BlockSpec(memory_space=pl.ANY)


def sketch_call(grad, test, old, first, second):
    rows, cols = grad.shape
    rank = test.shape[1]
    deep = 512
    block, small = rows // 8, rows // 32
    strip = rank // SIDE
    own_rank, tiles = first.shape[0], cols // 128
    leg = (2, SIDE, strip, 128)
    leg2 = (2, SIDE, strip // SIDE, 128)
    whole = (2, SIDE, SIDE, strip // SIDE, 128)
    buf = lambda *shape: pltpu.VMEM(shape, f32)
    return pl.pallas_call(
        functools.partial(sketch_kernel, tiles),
        out_shape=(
            jax.ShapeDtypeStruct((2, 2) + whole, f32),
            jax.ShapeDtypeStruct((2, SIDE, SIDE, small, rank), f32),
            jax.ShapeDtypeStruct((2, 32, own_rank, 128), f32),
        ),
        in_specs=[ANY, ANY, ANY, VMEM, VMEM],
        out_specs=(VMEM, VMEM, VMEM),
        scratch_shapes=[
            pltpu.VMEM((4, 2, block, cols), bf16),
            pltpu.VMEM((cols // deep, deep, rank), jnp.int32),
            pltpu.VMEM((cols // deep, deep, rank), bf16),
            buf(4, 2, block, rank),
            buf(2, 2, block // 2, rank),
            buf(2, 2, block, rank),
            buf(2, SIDE, small, rank),
            buf(2, 3, small, rank),
            buf(2, small, rank),
            buf(2, small, rank),
            buf(2, 2, *leg),
            buf(2, *leg),
            buf(2, *leg),
            buf(2, 3, 2, strip, 128),
            buf(2, *leg2),
            buf(2, 3, 2, strip // SIDE, 128),
            buf(2, 2, strip // SIDE, 128),
            buf(2, 3, 2, strip // SIDE, 128),
            buf(2, 2, strip // SIDE, 128),
            buf(2, *leg2),
            buf(2, *whole),
            pltpu.SemaphoreType.DMA((64,)),
            pltpu.SemaphoreType.DMA((64,)),
            pltpu.SemaphoreType.DMA((2, 32)),
            pltpu.SemaphoreType.DMA((2, 32)),
            pltpu.SemaphoreType.DMA((32,)),
        ],
        compiler_params=pltpu.CompilerParams(collective_id=0, has_side_effects=True),
    )(
        grad.reshape(2, SIDE, block, cols),
        test.reshape(cols // deep, deep, rank),
        old.reshape(2, SIDE, SIDE, small, rank),
        first,
        second,
    )


def factor_kernel(gh_ref, mc_ref, inv_ref, turned_ref):
    size = 128
    rank = inv_ref.shape[0]
    for part in range(rank // size):
        inv_ref[:, part * size : part * size + size] = gh_ref[part // 2, part % 2, 0].reshape(rank, size)
    inverse_factor(inv_ref)
    inverse = inv_ref[...]
    mixed = jnp.concatenate([gh_ref[p // 2, p % 2, 1].reshape(rank, size) for p in range(rank // size)], axis=1)
    corr = jnp.dot(inverse, mixed, precision=HI, preferred_element_type=f32)
    shape = turned_ref.shape[1:]
    old = mc_ref[0].reshape(rank, size)
    turned_ref[0] = jnp.dot(corr, old, precision=HI, preferred_element_type=f32).reshape(shape)
    old = mc_ref[1].reshape(rank, size)
    turned_ref[1] = jnp.dot(corr * corr, old, precision=HI, preferred_element_type=f32).reshape(shape)


def factor_call(gh, mc):
    rank = mc.shape[1] * mc.shape[2]
    return pl.pallas_call(
        factor_kernel,
        out_shape=(jax.ShapeDtypeStruct((rank, rank), f32), jax.ShapeDtypeStruct(mc.shape, f32)),
        in_specs=[VMEM, VMEM],
        out_specs=(VMEM, VMEM),
    )(gh, mc)


LAGS = (1, 2, 3, 4)


def project_kernel(
    tiles, bt_ref, g_hbm, turned_ref, proj_ref, first_ref, second_ref,
    g_buf, x_buf, core_in, y_buf, r_half, r_full, t_buf, last, t_in,
    send, recv, tsend, trecv, local_sem,
):
    at = place()
    c = at["c"]
    me = at["y"] * 8 + at["z"] * 2 + c
    links = Links(at, send, recv)
    barrier, count = greet(at, "", True)
    blocks = g_buf.shape[0]
    wide = g_buf.shape[2]
    cut = wide // 2
    axes = (("y", "z"), ("z", "y"))

    loads = []
    for b in range(blocks):
        out = pltpu.make_async_copy(g_hbm.at[:, pl.ds(b * wide, wide)], g_buf.at[b], local_sem.at[b])
        out.start()
        loads.append(out)

    def give(step):
        to, source = lax.rem(me + step, 32), lax.rem(me + (32 - step), 32)
        col = pl.ds(pl.multiple_of(lax.rem(me, tiles) * 128, 128), 128)
        return pltpu.make_async_remote_copy(
            src_ref=turned_ref.at[:, to],
            dst_ref=t_in.at[:, :, col],
            send_sem=tsend.at[step],
            recv_sem=trecv.at[step],
            device_id=device({**at, **plane_place(to)}),
            device_id_type=MESH,
        ), source

    def give_start(step, carry):
        out, source = give(step)
        pl.when(me < tiles)(functools.partial(begin, out))
        return carry

    def give_end(step, carry):
        out, source = give(step)
        pl.when(me < tiles)(functools.partial(sent, out))
        pl.when(source < tiles)(functools.partial(came, out))
        return carry

    across, firsts, fulls, lasts = {}, {}, {}, {}

    def multiply(b):
        loads[b].wait()
        out = jnp.dot(bt_ref[...], g_buf[b], preferred_element_type=f32)
        x_buf[b] = out.reshape(x_buf.shape[1:])
        if b == 0:
            pl.semaphore_wait(barrier, count)
        across[b] = links.copy(x_buf.at[b, :, :, 1 - c], core_in.at[b], "c", 1)

    def start_ring(b):
        across[b].wait_recv()
        total = x_buf[b, :, :, c] + core_in[b]
        y_buf[b, 0] = total[..., :cut]
        for i in range(SIDE):
            y_buf[b, 1, :, i] = total[i, :, :, cut:]
        for colour in range(2):
            axis = axes[colour][0]
            far = lax.rem(at[axis] + 2, SIDE)
            firsts[b, colour] = (
                links.copy(y_buf.at[b, colour, far, pl.ds(0, 2)], r_half.at[b, colour, 0], axis, 1),
                links.copy(y_buf.at[b, colour, far, pl.ds(2, 2)], r_half.at[b, colour, 1], axis, -1),
            )

    def pass_on(b):
        for colour in range(2):
            axis = axes[colour][0]
            outs = []
            for side in range(2):
                firsts[b, colour][side].wait_recv()
                to = lax.rem(at[axis] + (1, 3)[side], SIDE)
                y_buf[b, colour, to, 2 * side : 2 * side + 2] += r_half[b, colour, side]
                outs.append(links.copy(y_buf.at[b, colour, to], r_full.at[b, colour, side], axis, (1, -1)[side]))
            fulls[b, colour] = outs

    def second_axis(b):
        for colour in range(2):
            axis, other = axes[colour]
            for out in fulls[b, colour]:
                out.wait_recv()
            t_buf[b, colour] = y_buf[b, colour, at[axis]] + (r_full[b, colour, 0] + r_full[b, colour, 1])
            lasts[b, colour] = [
                links.copy(
                    t_buf.at[b, colour, lax.rem(at[other] + step, SIDE)], last.at[b, colour, step - 1], other, step
                )
                for step in (1, 2, 3)
            ]

    def complete(b):
        for colour in range(2):
            for out in lasts[b, colour]:
                out.wait_recv()
            start = b * wide + colour * cut
            proj_ref[:, start : start + cut] = tree(t_buf[b, colour, at[axes[colour][1]]], last[b, colour])

    jobs = (start_ring, pass_on, second_axis, complete)
    for tick in range(blocks + LAGS[-1]):
        if tick < blocks:
            multiply(tick)
        if tick == 0:
            lax.fori_loop(1, 32, give_start, 0)
        for job, lag in reversed(tuple(zip(jobs, LAGS))):
            if 0 <= tick - lag < blocks:
                job(tick - lag)

    @pl.when(me < tiles)
    def _():
        col = pl.ds(pl.multiple_of(lax.rem(me, tiles) * 128, 128), 128)
        t_in[:, :, col] = turned_ref[:, me]

    lax.fori_loop(1, 32, give_end, 0)
    total = proj_ref[...]
    first_ref[...] = 0.9 * t_in[0] + 0.1 * total
    second_ref[...] = 0.95 * t_in[1] + 0.05 * total * total
    links.finish()


def project_call(bt, grad, turned):
    rank, rows = bt.shape
    cols = grad.shape[1]
    own = turned.shape[2]
    wide = 512
    blocks = cols // wide
    cut = wide // 2
    out = jax.ShapeDtypeStruct((own, cols), f32)
    buf = lambda *shape: pltpu.VMEM(shape, f32)
    return pl.pallas_call(
        functools.partial(project_kernel, cols // 128),
        out_shape=(out, out, out),
        in_specs=[VMEM, ANY, VMEM],
        out_specs=(VMEM, VMEM, VMEM),
        scratch_shapes=[
            pltpu.VMEM((blocks, rows, wide), bf16),
            buf(blocks, SIDE, SIDE, 2, own, wide),
            buf(blocks, SIDE, SIDE, own, wide),
            buf(blocks, 2, SIDE, SIDE, own, cut),
            buf(blocks, 2, 2, 2, own, cut),
            buf(blocks, 2, 2, SIDE, own, cut),
            buf(blocks, 2, SIDE, own, cut),
            buf(blocks, 2, 3, own, cut),
            buf(2, own, cols),
            pltpu.SemaphoreType.DMA((15 * blocks,)),
            pltpu.SemaphoreType.DMA((15 * blocks,)),
            pltpu.SemaphoreType.DMA((32,)),
            pltpu.SemaphoreType.DMA((32,)),
            pltpu.SemaphoreType.DMA((blocks,)),
        ],
        compiler_params=pltpu.CompilerParams(collective_id=1, has_side_effects=True),
    )(bt, grad, turned)


def local(gradients, test_matrix, old_basis, first_moment, second_moment):
    grad = gradients[0]
    gh, sketch, columns = sketch_call(grad, test_matrix, old_basis, first_moment, second_moment)
    inverse, turned = factor_call(gh, columns)
    sketch = sketch.reshape(grad.shape[0], -1)
    basis = lax.dot_general(inverse, sketch, (((1,), (1,)), ((), ())), precision=HI, preferred_element_type=f32)
    return project_call(basis.astype(bf16), grad, turned)


def solution(mesh):
    moment = P(("dp", "row"), "col")
    in_specs = (P("dp", "row", "col"), P("col", None), P("row", None), moment, moment)
    return jax.shard_map(local, mesh=mesh, in_specs=in_specs, out_specs=(moment,) * 3, check_vma=False)
```

```python
import functools
import jax, jax.numpy as jnp
from jax import lax
from jax.experimental import pallas as pl
from jax.experimental.pallas import tpu as pltpu
from jax.sharding import PartitionSpec as P

HI = lax.Precision.HIGHEST
f32 = jnp.float32


def factor_diag(block, group):
    size = block.shape[0]
    tiles = size // 8
    z = [block[8 * b : 8 * b + 8, :] for b in range(tiles)]
    lane = lax.broadcasted_iota(jnp.int32, (8, size), 1)
    sub = lax.broadcasted_iota(jnp.int32, (8, size), 0)
    full = lambda v: jnp.broadcast_to(v, (8, size))
    for b in range(tiles):
        pivots = jnp.ones((8, size), f32)
        for r in range(0, 8, group):
            j = 8 * b + r
            piv = [[full(z[b][r + t : r + t + 1, j + s : j + s + 1]) for s in range(group)] for t in range(group)]
            inside = (lane >= j) & (lane < j + group)
            rows = [
                jnp.where(inside, (lane == j + t).astype(f32), full(z[b][r + t : r + t + 1, :])) for t in range(group)
            ]
            inv = []
            for t in range(group):
                pivots = jnp.where(sub == r + t, piv[t][t], pivots)
                inv.append(1.0 / piv[t][t])
                for u in range(t + 1, group):
                    m = piv[t][u] * inv[t]
                    for s in range(u, group):
                        piv[u][s] = piv[u][s] - m * piv[t][s]
                    rows[u] = rows[u] - m * rows[t]
            for i in range(b, tiles):
                cols = [full_col(z[i], j + t, size) for t in range(group)]
                acc = jnp.where(inside, (sub - r == lane - j).astype(f32) if i == b else 0.0, z[i])
                for t in range(group):
                    m = cols[t] * inv[t]
                    for u in range(t + 1, group):
                        cols[u] = cols[u] - m * piv[t][u]
                    if i == b:
                        m = jnp.where(sub > r + t, m, 0.0)
                    acc = acc - m * rows[t]
                z[i] = acc
        z[b] = z[b] * lax.rsqrt(pivots)
    out = jnp.concatenate(z, axis=0)
    i = lax.broadcasted_iota(jnp.int32, (size, size), 0)
    k = lax.broadcasted_iota(jnp.int32, (size, size), 1)
    return jnp.where(k <= i, out, 0.0)


def full_col(tile, j, size):
    return jnp.broadcast_to(tile[:, j : j + 1], (8, size))


def inverse_factor(z, group=8, size=128, ticks=()):
    n = z.shape[0]
    blocks = n // size
    for k in range(blocks):
        at = slice(k * size, k * size + size)
        inv = factor_diag(z[at, at], group)
        z[at, :] = jnp.dot(inv, z[at, :], precision=HI, preferred_element_type=f32)
        z[at, at] = inv
        if 2 * k < len(ticks):
            ticks[2 * k]()
        if k + 1 < blocks:
            below = slice(k * size + size, n)
            low = z[at, below]
            z[below, at] = jnp.zeros((n - below.start, size), f32)
            z[below, :] = z[below, :] - lax.dot_general(
                low, z[at, :], (((0,), (0,)), ((), ())), precision=HI, preferred_element_type=f32
            )
        if 2 * k + 1 < len(ticks):
            ticks[2 * k + 1]()
    row = lax.broadcasted_iota(jnp.int32, (n, n), 0) // size
    col = lax.broadcasted_iota(jnp.int32, (n, n), 1) // size
    z[...] = jnp.where(col <= row, z[...], 0.0)
MESH = pl.DeviceIdType.MESH
bf16 = jnp.bfloat16
SIDE = 4
VMEM = pl.BlockSpec(memory_space=pltpu.VMEM)
ANY = pl.BlockSpec(memory_space=pl.ANY)
LAGS = (1, 3, 5, 7)
TURN = 3


def plane_place(p):
    return {"y": p // 8, "z": (p // 2) % 4, "c": p % 2}


def device(at):
    return (at["y"], at["z"] * 2 + at["c"], at["x"])


class Place:
    def __init__(self):
        row = lax.axis_index("row")
        self.at = {"x": lax.axis_index("col"), "y": lax.axis_index("dp"), "z": row // 2, "c": row % 2}
        self.rank = self.at["y"] * 8 + row
        self.near, self.devices = {}, {}
        for axis, here in self.at.items():
            size = 2 if axis == "c" else SIDE
            for step in range(size):
                there = lax.rem(here + step, size)
                self.near[axis, step] = there
                self.devices[axis, step] = device({**self.at, axis: there})

    def __getitem__(self, axis):
        return self.at[axis]

    def of(self, axis, step):
        return self.near[axis, step % SIDE]


class Copy:
    def __init__(self, links, src, dst, axis, step, number):
        self.links, self.src, self.dst, self.number = links, src, dst, number
        self.device = links.place.devices[axis, step % (2 if axis == "c" else SIDE)]

    def build(self):
        src, dst = (ref[0].at[ref[1]] if isinstance(ref, tuple) else ref for ref in (self.src, self.dst))
        return pltpu.make_async_remote_copy(
            src_ref=src,
            dst_ref=dst,
            send_sem=self.links.send.at[self.number],
            recv_sem=self.links.recv.at[self.number],
            device_id=self.device,
            device_id_type=MESH,
        )

    def wait_recv(self):
        self.build().wait_recv()

    def wait_send(self):
        self.build().wait_send()


class Links:
    def __init__(self, place, send, recv):
        self.place, self.send, self.recv, self.used, self.started = place, send, recv, 0, []

    def copy(self, src, dst, axis, step):
        out = Copy(self, src, dst, axis, step, self.used)
        self.used += 1
        self.started.append(out)
        out.build().start()
        return out

    def finish(self):
        for out in self.started:
            out.wait_send()


def begin(out):
    out.start()


def sent(out):
    out.wait_send()


def came(out):
    out.wait_recv()


def arrive(outs):
    for out in outs:
        out.wait_recv()


def tree(own, slots):
    return (own + slots[1]) + (slots[0] + slots[2])


def split3(value):
    high = value.astype(bf16)
    rest = value - high.astype(f32)
    mid = rest.astype(bf16)
    low = (rest - mid.astype(f32)).astype(bf16)
    return high, mid, low


class Total:
    orders = (("x", "y", "z"), ("y", "z", "x"))

    def __init__(self, place, links, parts, core_in, v0, r1, v1, r2, v2, r3, v3, w1, w0, out):
        self.place, self.links, self.parts, self.core_in, self.out = place, links, parts, core_in, out
        self.v0, self.r1, self.v1, self.r2, self.v2 = v0, r1, v1, r2, v2
        self.r3, self.v3, self.w1, self.w0 = r3, v3, w1, w0
        self.flying = []

    def steps(self):
        return (self.core, self.first, self.second, self.third, self.back2, self.back1, self.join, self.end)

    def core(self):
        self.flying = [self.links.copy(self.parts.at[1 - self.place["c"]], self.core_in, "c", 1)]

    def send(self, level, src, dst):
        arrivals = []
        for colour in range(2):
            axis = self.orders[colour][level]
            for step in (1, 2, 3):
                arrivals.append(self.links.copy(src(colour, axis, step), dst(colour, axis, step), axis, step))
        self.flying = arrivals

    def first(self):
        arrive(self.flying)
        self.v0[...] = self.parts[self.place["c"]] + self.core_in[...]
        self.send(
            0,
            lambda colour, axis, step: self.v0.at[colour, self.place.of(axis, step)],
            lambda colour, axis, step: self.r1.at[colour, step - 1],
        )

    def second(self):
        arrive(self.flying)
        for colour in range(2):
            mine = self.v0[colour, self.place[self.orders[colour][0]]]
            self.v1[colour] = tree(mine, self.r1[colour]).reshape(self.v1.shape[1:])
        self.send(
            1,
            lambda colour, axis, step: self.v1.at[colour, self.place.of(axis, step)],
            lambda colour, axis, step: self.r2.at[colour, step - 1],
        )

    def third(self):
        arrive(self.flying)
        for colour in range(2):
            self.v2[colour] = tree(self.v1[colour, self.place[self.orders[colour][1]]], self.r2[colour])
        self.send(
            2,
            lambda colour, axis, step: self.v2.at[colour],
            lambda colour, axis, step: self.r3.at[colour, step - 1],
        )

    def back2(self):
        arrive(self.flying)
        for colour in range(2):
            total = tree(self.v2[colour], self.r3[colour])
            self.v3[colour] = total
            self.w1[colour, self.place[self.orders[colour][1]]] = total
        self.send(
            1,
            lambda colour, axis, step: self.v3.at[colour],
            lambda colour, axis, step: self.w1.at[colour, self.place[axis]],
        )

    def back1(self):
        arrive(self.flying)
        for colour in range(2):
            self.w0[colour, self.place[self.orders[colour][0]]] = self.w1[colour]
        self.send(
            0,
            lambda colour, axis, step: self.w1.at[colour],
            lambda colour, axis, step: self.w0.at[colour, self.place[axis]],
        )

    def join(self):
        arrive(self.flying)
        c = self.place["c"]
        self.out[c] = self.w0[...]
        self.flying = [self.links.copy(self.w0, self.out.at[c], "c", 1)]

    def end(self):
        arrive(self.flying)


def kernel(
    tiles, g_hbm, t_hbm, o_hbm, m1_ref, m2_ref, pa_ref, pb_ref, tin_ref,
    g_buf, t_buf, t_low, part, half, full, quarter, second, own, o_buf,
    parts, core_in, v0, r1, v1, r2, v2, r3, v3, w1, w0, totals,
    s_buf, mc_buf, z_buf, turned, b_low,
    x_buf, x_in, y_buf, r_half, r_full, p_buf, p_in,
    send, recv, msend, mrecv, tsend, trecv, local_sem,
):
    place = Place()
    x, y, c, me = place["x"], place["y"], place["c"], place.rank
    links = Links(place, send, recv)
    first_axis = ("x", "y")

    barrier = pltpu.get_barrier_semaphore()

    def greet(step, carry):
        to = {**place.at, **plane_place(lax.rem(me + step, 32))}
        pl.semaphore_signal(barrier, inc=1, device_id=device(to), device_id_type=MESH)
        return carry

    for step in (1, 2, 3):
        pl.semaphore_signal(barrier, inc=1, device_id=place.devices["x", step], device_id_type=MESH)
    lax.fori_loop(1, 32, greet, 0)

    loads = []

    def load(src, dst):
        out = pltpu.make_async_copy(src, dst, local_sem.at[len(loads)])
        out.start()
        loads.append(out)
        return out

    steps = (2, 1, -1, 0)
    chunks, deep, wide = t_buf.shape
    rows = g_buf.shape[2]
    g_loads, t_loads = {}, {}

    def load_g(i):
        g_loads[i] = [
            load(g_hbm.at[colour, place.of(first_axis[colour], steps[i])], g_buf.at[i, colour]) for colour in range(2)
        ]

    load_g(0)
    for k in range(chunks):
        t_loads[k] = load(t_hbm.at[k], t_buf.at[k])
    for i in (1, 2, 3):
        load_g(i)
    o_loads = [load(o_hbm.at[0, x, y], o_buf.at[0]), load(o_hbm.at[1, y, x], o_buf.at[1])]

    def product(i, k):
        lhs = g_buf[i, :, :, pl.ds(pl.multiple_of(k * deep, deep), deep)].reshape(2 * rows, deep)
        return jnp.dot(lhs, t_low[k], preferred_element_type=f32).reshape(2, rows, wide)

    def matmul(i):
        for out in g_loads[i]:
            out.wait()
        if i == 0:
            for k in range(chunks):
                t_loads[k].wait()
                t_low[k] = t_buf[k].astype(f32).astype(bf16)
                part[i] = product(i, k) + (part[i] if k else 0.0)
        else:
            part[i] = product(i, 0)

            def more(k, carry):
                part[i] += product(i, k)
                return carry

            lax.fori_loop(1, chunks, more, 0)

    matmul(0)
    pl.semaphore_wait(barrier, 34)
    mid = rows // 2
    up, down, ups, downs, later = [], [], [], [], []
    for colour, axis in enumerate(first_axis):
        up.append(links.copy(part.at[0, colour, pl.ds(0, mid)], half.at[0, colour], axis, 1))
        down.append(links.copy(part.at[0, colour, pl.ds(mid, mid)], half.at[1, colour], axis, -1))
    matmul(1)
    for colour, axis in enumerate(first_axis):
        up[colour].wait_recv()
        part[1, colour, 0:mid] += half[0, colour]
        ups.append(links.copy(part.at[1, colour], full.at[0, colour], axis, 1))
    matmul(2)
    for colour, axis in enumerate(first_axis):
        down[colour].wait_recv()
        part[2, colour, mid:] += half[1, colour]
        downs.append(links.copy(part.at[2, colour], full.at[1, colour], axis, -1))
    matmul(3)
    for colour, axis in enumerate(first_axis):
        other = first_axis[1 - colour]
        arrive((ups[colour], downs[colour]))
        total = part[3, colour] + (full[0, colour] + full[1, colour])
        quarter[colour] = total.reshape(quarter.shape[1:])
        later.append(
            [
                links.copy(quarter.at[colour, place.of(other, step)], second.at[colour, step - 1], other, step)
                for step in (1, 2, 3)
            ]
        )
    for colour in range(2):
        arrive(later[colour])
        own[colour] = tree(quarter[colour, place[first_axis[1 - colour]]], second[colour])

    mine = own[...].reshape(-1, wide)
    h, m, l = split3(mine)
    left = jnp.concatenate([h, h, m, h, m, l], axis=0)

    def share(value, kind):
        for core in range(2):
            a, b, e = split3(value[:, core * 256 : core * 256 + 256])
            right = jnp.concatenate([a, b, a, e, b, a], axis=0)
            out = lax.dot_general(left, right, (((0,), (0,)), ((), ())), preferred_element_type=f32)
            for colour in range(2):
                parts[kind, core, colour] = out[:, colour * 128 : colour * 128 + 128].reshape(parts.shape[3:])

    grams, mixes = (
        Total(
            place, links, parts.at[kind], core_in.at[kind], v0.at[kind], r1.at[kind], v1.at[kind], r2.at[kind],
            v2.at[kind], r3.at[kind], v3.at[kind], w1.at[kind], w0.at[kind], totals.at[kind],
        )
        for kind in range(2)
    )
    share(mine, 0)
    grams.core()
    for out in o_loads:
        out.wait()
    share(o_buf[...].reshape(-1, wide), 1)
    grams.first()
    mixes.core()
    grams.second()
    grams.third()
    grams.back2()
    grams.back1()
    grams.join()

    gather, ring, relay = [], [], []

    def gather_first():
        for colour in range(2):
            axis, other = first_axis[colour], first_axis[1 - colour]
            s_buf[colour, place[axis], place[other]] = own[colour]
            here = s_buf.at[colour, place[axis], place[other]]
            gather.extend(links.copy(own.at[colour], here, other, step) for step in (1, 2, 3))

    def gather_ring():
        arrive(gather)
        for colour, axis in enumerate(first_axis):
            here = s_buf.at[colour, place[axis]]
            ring.extend((links.copy(here, here, axis, 1), links.copy(here, here, axis, -1)))

    def gather_relay():
        arrive(ring)
        for colour, axis in enumerate(first_axis):
            low = s_buf.at[colour, place.of(axis, -1), pl.ds(0, 2)]
            high = s_buf.at[colour, place.of(axis, 1), pl.ds(2, 2)]
            relay.extend((links.copy(low, low, axis, 1), links.copy(high, high, axis, -1)))

    def trade(step, moment):
        to = lax.rem(me + step, 32)
        col = pl.ds(pl.multiple_of(lax.rem(to, tiles) * 128, 128), 128)
        return pltpu.make_async_remote_copy(
            src_ref=(m1_ref, m2_ref)[moment].at[:, col],
            dst_ref=mc_buf.at[moment, me],
            send_sem=msend.at[moment, step],
            recv_sem=mrecv.at[moment, step],
            device_id=device({**place.at, **plane_place(to)}),
            device_id_type=MESH,
        ), to

    def trade_start(step, carry):
        for moment in range(2):
            out, to = trade(step, moment)
            pl.when(to < tiles)(functools.partial(begin, out))
        return carry

    def trade_end(step, carry):
        for moment in range(2):
            out, to = trade(step, moment)
            pl.when(to < tiles)(functools.partial(sent, out))
            pl.when(me < tiles)(functools.partial(came, out))
        return carry

    own_col = pl.ds(pl.multiple_of(lax.rem(me, tiles) * 128, 128), 128)
    gather_first()
    lax.fori_loop(1, 32, trade_start, 0)
    mc_buf[0, me] = m1_ref[:, own_col]
    mc_buf[1, me] = m2_ref[:, own_col]
    grams.end()

    size = 128
    rank = z_buf.shape[0]
    for p in range(rank // size):
        z_buf[:, p * size : p * size + size] = totals[0, p // 2, p % 2].reshape(rank, size)

    mix = mixes.steps()

    def both(*jobs):
        def run():
            for job in jobs:
                job()

        return run

    inverse_factor(
        z_buf,
        ticks=(
            both(mix[1]),
            both(gather_ring),
            both(mix[2]),
            both(mix[3], gather_relay),
            both(mix[4]),
            both(mix[5]),
            both(mix[6]),
            both(mix[7]),
        ),
    )
    arrive(relay)

    blocks = x_buf.shape[0]
    stack = [
        s_buf[colour, place.of(first_axis[colour], steps[i])].reshape(rows, rank) for i in range(4) for colour in range(2)
    ]
    whole = jnp.concatenate(stack, axis=0)
    middle = rank // 2
    dims = (((1,), (1,)), ((), ()))
    for start in (0, middle):
        deep_end = start + middle
        b_low[start:deep_end] = lax.dot_general(
            z_buf[start:deep_end, 0:deep_end], whole[:, 0:deep_end], dims, precision=HI, preferred_element_type=f32
        ).astype(bf16)

    width = x_buf.shape[-1]
    cut = width // 2
    axes = (("y", "z"), ("z", "y"))
    across, firsts, fulls, lasts = {}, {}, {}, {}

    def multiply(b):
        block = g_buf[:, :, :, b * width : b * width + width].reshape(8 * rows, width)
        out = jnp.dot(b_low[...], block, preferred_element_type=f32)
        x_buf[b] = out.reshape(x_buf.shape[1:])
        across[b] = links.copy(x_buf.at[b, :, :, 1 - c], x_in.at[b], "c", 1)

    def start_ring(b):
        across[b].wait_recv()
        total = x_buf[b, :, :, c] + x_in[b]
        y_buf[b, 0] = total[..., :cut]
        for i in range(SIDE):
            y_buf[b, 1, :, i] = total[i, :, :, cut:]
        for colour in range(2):
            axis = axes[colour][0]
            far = place.of(axis, 2)
            firsts[b, colour] = (
                links.copy(y_buf.at[b, colour, far, pl.ds(0, 2)], r_half.at[b, colour, 0], axis, 1),
                links.copy(y_buf.at[b, colour, far, pl.ds(2, 2)], r_half.at[b, colour, 1], axis, -1),
            )

    def pass_on(b):
        for colour in range(2):
            axis = axes[colour][0]
            outs = []
            for side in range(2):
                firsts[b, colour][side].wait_recv()
                to = place.of(axis, (1, -1)[side])
                y_buf[b, colour, to, 2 * side : 2 * side + 2] += r_half[b, colour, side]
                outs.append(links.copy(y_buf.at[b, colour, to], r_full.at[b, colour, side], axis, (1, -1)[side]))
            fulls[b, colour] = outs

    def second_axis(b):
        for colour in range(2):
            axis, other = axes[colour]
            arrive(fulls[b, colour])
            p_buf[b, colour] = y_buf[b, colour, place[axis]] + (r_full[b, colour, 0] + r_full[b, colour, 1])
            lasts[b, colour] = [
                links.copy(p_buf.at[b, colour, place.of(other, step)], p_in.at[b, colour, step - 1], other, step)
                for step in (1, 2, 3)
            ]

    def complete(b):
        for colour in range(2):
            arrive(lasts[b, colour])
            start = b * width + colour * cut
            pa_ref[:, start : start + cut] = p_buf[b, colour, place[axes[colour][1]]] + p_in[b, colour, 1]
            pb_ref[:, start : start + cut] = p_in[b, colour, 0] + p_in[b, colour, 2]

    def give(step):
        to, source = lax.rem(me + step, 32), lax.rem(me + (32 - step), 32)
        return pltpu.make_async_remote_copy(
            src_ref=turned.at[:, to],
            dst_ref=tin_ref.at[:, :, own_col],
            send_sem=tsend.at[step],
            recv_sem=trecv.at[step],
            device_id=device({**place.at, **plane_place(to)}),
            device_id_type=MESH,
        ), source

    def give_start(step, carry):
        out, source = give(step)
        pl.when(me < tiles)(functools.partial(begin, out))
        return carry

    def give_end(step, carry):
        out, source = give(step)
        pl.when(me < tiles)(functools.partial(sent, out))
        pl.when(source < tiles)(functools.partial(came, out))
        return carry

    def turn():
        lax.fori_loop(1, 32, trade_end, 0)
        mixed = jnp.concatenate([totals[1, p // 2, p % 2].reshape(rank, size) for p in range(rank // size)], axis=1)
        corr = jnp.dot(z_buf[...], mixed, precision=HI, preferred_element_type=f32)
        shape = turned.shape[1:]
        old = mc_buf[0].reshape(rank, size)
        turned[0] = jnp.dot(corr, old, precision=HI, preferred_element_type=f32).reshape(shape)
        old = mc_buf[1].reshape(rank, size)
        turned[1] = jnp.dot(corr * corr, old, precision=HI, preferred_element_type=f32).reshape(shape)
        lax.fori_loop(1, 32, give_start, 0)

        @pl.when(me < tiles)
        def _():
            tin_ref[:, :, own_col] = turned[:, me]

    jobs = tuple(zip((start_ring, pass_on, second_axis, complete), LAGS))
    for tick in range(blocks + LAGS[-1]):
        if tick < blocks:
            multiply(tick)
        for job, lag in reversed(jobs):
            if 0 <= tick - lag < blocks:
                job(tick - lag)
        if tick == TURN:
            turn()
    lax.fori_loop(1, 32, give_end, 0)
    links.finish()


def call(grad, test, old, first, second):
    rows, cols = grad.shape
    rank = test.shape[1]
    deep = 512
    block, small = rows // 8, rows // 32
    strip = rank // SIDE
    bit = strip // SIDE
    own_rank, tiles = first.shape[0], cols // 128
    width = 512
    blocks = cols // width
    cut = width // 2
    buf = lambda *shape: pltpu.VMEM(shape, f32)
    dma = lambda *shape: pltpu.SemaphoreType.DMA(shape)
    copies = 24 + 2 * 40 + 16 + 15 * blocks
    out = jax.ShapeDtypeStruct((own_rank, cols), f32)
    return pl.pallas_call(
        functools.partial(kernel, tiles),
        out_shape=(out, out, jax.ShapeDtypeStruct((2, own_rank, cols), f32)),
        in_specs=[ANY, ANY, ANY, VMEM, VMEM],
        out_specs=(VMEM, VMEM, VMEM),
        scratch_shapes=[
            pltpu.VMEM((4, 2, block, cols), bf16),
            pltpu.VMEM((cols // deep, deep, rank), jnp.int32),
            pltpu.VMEM((cols // deep, deep, rank), bf16),
            buf(4, 2, block, rank),
            buf(2, 2, block // 2, rank),
            buf(2, 2, block, rank),
            buf(2, SIDE, small, rank),
            buf(2, 3, small, rank),
            buf(2, small, rank),
            buf(2, small, rank),
            buf(2, 2, 2, SIDE, strip, 128),
            buf(2, 2, SIDE, strip, 128),
            buf(2, 2, SIDE, strip, 128),
            buf(2, 2, 3, strip, 128),
            buf(2, 2, SIDE, bit, 128),
            buf(2, 2, 3, bit, 128),
            buf(2, 2, bit, 128),
            buf(2, 2, 3, bit, 128),
            buf(2, 2, bit, 128),
            buf(2, 2, SIDE, bit, 128),
            buf(2, 2, SIDE, SIDE, bit, 128),
            buf(2, 2, 2, SIDE, SIDE, bit, 128),
            buf(2, SIDE, SIDE, small, rank),
            buf(2, 32, own_rank, 128),
            buf(rank, rank),
            buf(2, 32, own_rank, 128),
            pltpu.VMEM((rank, rows), bf16),
            buf(blocks, SIDE, SIDE, 2, own_rank, width),
            buf(blocks, SIDE, SIDE, own_rank, width),
            buf(blocks, 2, SIDE, SIDE, own_rank, cut),
            buf(blocks, 2, 2, 2, own_rank, cut),
            buf(blocks, 2, 2, SIDE, own_rank, cut),
            buf(blocks, 2, SIDE, own_rank, cut),
            buf(blocks, 2, 3, own_rank, cut),
            dma(copies),
            dma(copies),
            dma(2, 32),
            dma(2, 32),
            dma(32),
            dma(32),
            dma(32),
        ],
        compiler_params=pltpu.CompilerParams(
            collective_id=0, has_side_effects=True, vmem_limit_bytes=67043328
        ),
    )(
        grad.reshape(2, SIDE, block, cols),
        test.reshape(cols // deep, deep, rank),
        old.reshape(2, SIDE, SIDE, small, rank),
        first,
        second,
    )


def local(gradients, test_matrix, old_basis, first_moment, second_moment):
    one, other, turned = call(gradients[0], test_matrix, old_basis, first_moment, second_moment)
    projected = one + other
    first_new = 0.9 * turned[0] + 0.1 * projected
    second_new = 0.95 * turned[1] + 0.05 * projected * projected
    return projected, first_new, second_new


def solution(mesh):
    moment = P(("dp", "row"), "col")
    in_specs = (P("dp", "row", "col"), P("col", None), P("row", None), moment, moment)
    return jax.shard_map(local, mesh=mesh, in_specs=in_specs, out_specs=(moment,) * 3, check_vma=False)
```

```python
import functools
import jax, jax.numpy as jnp
from jax import lax
from jax.experimental import pallas as pl
from jax.experimental.pallas import tpu as pltpu
from jax.sharding import PartitionSpec as P

HI = lax.Precision.HIGHEST
f32 = jnp.float32


def factor_diag(block, group, middle=None):
    size = block.shape[0]
    tiles = size // 8
    z = [block[8 * b : 8 * b + 8, :] for b in range(tiles)]
    lane = lax.broadcasted_iota(jnp.int32, (8, size), 1)
    sub = lax.broadcasted_iota(jnp.int32, (8, size), 0)
    full = lambda v: jnp.broadcast_to(v, (8, size))
    for b in range(tiles):
        if b == tiles // 2 and middle is not None:
            middle()
        pivots = jnp.ones((8, size), f32)
        for r in range(0, 8, group):
            j = 8 * b + r
            piv = [[full(z[b][r + t : r + t + 1, j + s : j + s + 1]) for s in range(group)] for t in range(group)]
            inside = (lane >= j) & (lane < j + group)
            rows = [
                jnp.where(inside, (lane == j + t).astype(f32), full(z[b][r + t : r + t + 1, :])) for t in range(group)
            ]
            inv = []
            for t in range(group):
                pivots = jnp.where(sub == r + t, piv[t][t], pivots)
                inv.append(1.0 / piv[t][t])
                for u in range(t + 1, group):
                    m = piv[t][u] * inv[t]
                    for s in range(u, group):
                        piv[u][s] = piv[u][s] - piv[t][u] * piv[t][s] * inv[t]
                    rows[u] = rows[u] - m * rows[t]
            for i in range(b, tiles):
                cols = [full_col(z[i], j + t, size) for t in range(group)]
                acc = jnp.where(inside, (sub - r == lane - j).astype(f32) if i == b else 0.0, z[i])
                for t in range(group):
                    m = cols[t] * inv[t]
                    for u in range(t + 1, group):
                        cols[u] = cols[u] - m * piv[t][u]
                    if i == b:
                        m = jnp.where(sub > r + t, m, 0.0)
                    acc = acc - m * rows[t]
                z[i] = acc
        z[b] = z[b] * lax.rsqrt(pivots)
    out = jnp.concatenate(z, axis=0)
    i = lax.broadcasted_iota(jnp.int32, (size, size), 0)
    k = lax.broadcasted_iota(jnp.int32, (size, size), 1)
    return jnp.where(k <= i, out, 0.0)


def full_col(tile, j, size):
    return jnp.broadcast_to(tile[:, j : j + 1], (8, size))


def inverse_factor(z, group=8, size=128, ticks=()):
    n = z.shape[0]
    blocks = n // size
    for k in range(blocks):
        at = slice(k * size, k * size + size)
        inv = factor_diag(z[at, at], group, ticks[2 * k] if ticks else None)
        z[at, :] = jnp.dot(inv, z[at, :], precision=HI, preferred_element_type=f32)
        z[at, at] = inv
        if k + 1 < blocks:
            below = slice(k * size + size, n)
            low = z[at, below]
            z[below, at] = jnp.zeros((n - below.start, size), f32)
            z[below, :] = z[below, :] - lax.dot_general(
                low, z[at, :], (((0,), (0,)), ((), ())), precision=HI, preferred_element_type=f32
            )
        if 2 * k + 1 < len(ticks):
            ticks[2 * k + 1]()
    row = lax.broadcasted_iota(jnp.int32, (n, n), 0) // size
    col = lax.broadcasted_iota(jnp.int32, (n, n), 1) // size
    z[...] = jnp.where(col <= row, z[...], 0.0)
MESH = pl.DeviceIdType.MESH
bf16 = jnp.bfloat16
SIDE = 4
VMEM = pl.BlockSpec(memory_space=pltpu.VMEM)
ANY = pl.BlockSpec(memory_space=pl.ANY)


def plane_place(p):
    return {"y": p // 8, "z": (p // 2) % 4, "c": p % 2}


def device(at):
    return (at["y"], at["z"] * 2 + at["c"], at["x"])


class Place:
    def __init__(self):
        row = lax.axis_index("row")
        self.at = {"x": lax.axis_index("col"), "y": lax.axis_index("dp"), "z": row // 2, "c": row % 2}
        self.rank = self.at["y"] * 8 + row
        self.near, self.devices = {}, {}
        for axis, here in self.at.items():
            size = 2 if axis == "c" else SIDE
            for step in range(size):
                there = lax.rem(here + step, size)
                self.near[axis, step] = there
                self.devices[axis, step] = device({**self.at, axis: there})

    def __getitem__(self, axis):
        return self.at[axis]

    def of(self, axis, step):
        return self.near[axis, step % SIDE]


class Copy:
    def __init__(self, links, src, dst, axis, step, number):
        self.links, self.src, self.dst, self.number = links, src, dst, number
        self.device = links.place.devices[axis, step % (2 if axis == "c" else SIDE)]

    def build(self):
        src, dst = (ref[0].at[ref[1]] if isinstance(ref, tuple) else ref for ref in (self.src, self.dst))
        return pltpu.make_async_remote_copy(
            src_ref=src,
            dst_ref=dst,
            send_sem=self.links.send.at[self.number],
            recv_sem=self.links.recv.at[self.number],
            device_id=self.device,
            device_id_type=MESH,
        )

    def wait_recv(self):
        self.build().wait_recv()

    def wait_send(self):
        self.build().wait_send()


class Links:
    def __init__(self, place, send, recv):
        self.place, self.send, self.recv, self.used, self.started = place, send, recv, 0, []

    def copy(self, src, dst, axis, step):
        out = Copy(self, src, dst, axis, step, self.used)
        self.used += 1
        self.started.append(out)
        out.build().start()
        return out

    def finish(self):
        for out in self.started:
            out.wait_send()


def begin(out):
    out.start()


def sent(out):
    out.wait_send()


def came(out):
    out.wait_recv()


def arrive(outs):
    for out in outs:
        out.wait_recv()


def tree(own, slots):
    return (own + slots[1]) + (slots[0] + slots[2])


def split3(value):
    high = value.astype(bf16)
    rest = value - high.astype(f32)
    mid = rest.astype(bf16)
    low = (rest - mid.astype(f32)).astype(bf16)
    return high, mid, low


class Total:
    orders = (("x", "z", "y"), ("y", "z", "x"))

    def __init__(self, place, links, parts, core_in, v0, r1, v1, r2, v2, r3, v3, w1, w0, out):
        self.place, self.links, self.parts, self.core_in, self.out = place, links, parts, core_in, out
        self.v0, self.r1, self.v1, self.r2, self.v2 = v0, r1, v1, r2, v2
        self.r3, self.v3, self.w1, self.w0 = r3, v3, w1, w0
        self.flying = []

    def steps(self):
        return (self.core, self.first, self.second, self.third, self.back2, self.back1, self.join, self.end)

    def core(self):
        self.flying = [self.links.copy(self.parts.at[1 - self.place["c"]], self.core_in, "c", 1)]

    def send(self, level, src, dst):
        arrivals = []
        for colour in range(2):
            axis = self.orders[colour][level]
            for step in (1, 2, 3):
                arrivals.append(self.links.copy(src(colour, axis, step), dst(colour, axis, step), axis, step))
        self.flying = arrivals

    def first(self):
        arrive(self.flying)
        self.v0[...] = self.parts[self.place["c"]] + self.core_in[...]
        self.send(
            0,
            lambda colour, axis, step: self.v0.at[colour, self.place.of(axis, step)],
            lambda colour, axis, step: self.r1.at[colour, step - 1],
        )

    def second(self):
        arrive(self.flying)
        for colour in range(2):
            mine = self.v0[colour, self.place[self.orders[colour][0]]]
            self.v1[colour] = tree(mine, self.r1[colour]).reshape(self.v1.shape[1:])
        self.send(
            1,
            lambda colour, axis, step: self.v1.at[colour, self.place.of(axis, step)],
            lambda colour, axis, step: self.r2.at[colour, step - 1],
        )

    def third(self):
        arrive(self.flying)
        for colour in range(2):
            self.v2[colour] = tree(self.v1[colour, self.place[self.orders[colour][1]]], self.r2[colour])
        self.send(
            2,
            lambda colour, axis, step: self.v2.at[colour],
            lambda colour, axis, step: self.r3.at[colour, step - 1],
        )

    def back2(self):
        arrive(self.flying)
        for colour in range(2):
            total = tree(self.v2[colour], self.r3[colour])
            self.v3[colour] = total
            self.w1[colour, self.place[self.orders[colour][1]]] = total
        self.send(
            1,
            lambda colour, axis, step: self.v3.at[colour],
            lambda colour, axis, step: self.w1.at[colour, self.place[axis]],
        )

    def back1(self):
        arrive(self.flying)
        for colour in range(2):
            self.w0[colour, self.place[self.orders[colour][0]]] = self.w1[colour]
        self.send(
            0,
            lambda colour, axis, step: self.w1.at[colour],
            lambda colour, axis, step: self.w0.at[colour, self.place[axis]],
        )

    def join(self):
        arrive(self.flying)
        c = self.place["c"]
        self.out[c] = self.w0[...]
        self.flying = [self.links.copy(self.w0, self.out.at[c], "c", 1)]

    def end(self):
        arrive(self.flying)


def kernel(
    tiles, g_hbm, t_hbm, o_hbm, m1_ref, m2_ref, pin_ref, tin_ref,
    g_buf, t_buf, t_low, part, half, full, quarter, second, own, o_buf,
    parts, core_in, v0, r1, v1, r2, v2, r3, v3, w1, w0, totals,
    s_buf, m_buf, mc_buf, z_buf, corr_buf, turned, made, st_buf,
    x_buf, x_in, y_buf, r_half, r_full, p_buf, p_in,
    send, recv, msend, mrecv, tsend, trecv, local_sem,
):
    place = Place()
    x, y, c, me = place["x"], place["y"], place["c"], place.rank
    links = Links(place, send, recv)
    first_axis = ("x", "y")

    barrier = pltpu.get_barrier_semaphore()

    def greet(step, carry):
        to = {**place.at, **plane_place(lax.rem(me + step, 32))}
        pl.semaphore_signal(barrier, inc=1, device_id=device(to), device_id_type=MESH)
        return carry

    loads = []

    def load(src, dst):
        out = pltpu.make_async_copy(src, dst, local_sem.at[len(loads)])
        out.start()
        loads.append(out)
        return out

    steps = (2, 1, -1, 0)
    chunks, deep, wide = t_buf.shape
    rows = g_buf.shape[2]
    g_loads, t_loads = {}, {}

    def load_g(i):
        g_loads[i] = [
            load(g_hbm.at[colour, place.of(first_axis[colour], steps[i])], g_buf.at[i, colour]) for colour in range(2)
        ]

    load_g(0)
    for k in range(chunks):
        t_loads[k] = load(t_hbm.at[k], t_buf.at[k])
    for i in (1, 2, 3):
        load_g(i)
    o_loads = [load(o_hbm.at[0, x, y], o_buf.at[0]), load(o_hbm.at[1, y, x], o_buf.at[1])]

    for step in (1, 2, 3):
        pl.semaphore_signal(barrier, inc=1, device_id=place.devices["x", step], device_id_type=MESH)
    lax.fori_loop(1, 32, greet, 0)

    def product(i, k):
        lhs = g_buf[i, :, :, pl.ds(pl.multiple_of(k * deep, deep), deep)].reshape(2 * rows, deep)
        return jnp.dot(lhs, t_low[k], preferred_element_type=f32).reshape(2, rows, wide)

    def matmul(i):
        for out in g_loads[i]:
            out.wait()
        if i == 0:
            for k in range(chunks):
                t_loads[k].wait()
                t_low[k] = t_buf[k].astype(f32).astype(bf16)
                part[i] = product(i, k) + (part[i] if k else 0.0)
        else:
            part[i] = product(i, 0)

            def more(k, carry):
                part[i] += product(i, k)
                return carry

            lax.fori_loop(1, chunks, more, 0)

    def trade(step):
        to = lax.rem(me + step, 32)
        col = pl.ds(pl.multiple_of(lax.rem(to, tiles) * 128, 128), 128)
        return pltpu.make_async_remote_copy(
            src_ref=m_buf.at[:, :, col],
            dst_ref=mc_buf.at[:, me],
            send_sem=msend.at[step],
            recv_sem=mrecv.at[step],
            device_id=device({**place.at, **plane_place(to)}),
            device_id_type=MESH,
        ), to

    def trade_start(step, carry):
        out, to = trade(step)
        pl.when(to < tiles)(functools.partial(begin, out))
        return carry

    def trade_end(step, carry):
        out, to = trade(step)
        pl.when(to < tiles)(functools.partial(sent, out))
        pl.when(me < tiles)(functools.partial(came, out))
        return carry

    own_col = pl.ds(pl.multiple_of(lax.rem(me, tiles) * 128, 128), 128)

    matmul(0)
    m_buf[0] = m1_ref[...]
    m_buf[1] = m2_ref[...]
    pl.semaphore_wait(barrier, 34)
    mid = rows // 2
    up, down, ups, downs, later = [], [], [], [], []
    for colour, axis in enumerate(first_axis):
        up.append(links.copy(part.at[0, colour, pl.ds(0, mid)], half.at[0, colour], axis, 1))
        down.append(links.copy(part.at[0, colour, pl.ds(mid, mid)], half.at[1, colour], axis, -1))
    matmul(1)
    low, high = pl.ds(0, mid), pl.ds(mid, mid)
    for colour, axis in enumerate(first_axis):
        ups.append(links.copy(part.at[1, colour, high], full.at[0, colour, high], axis, 1))
    matmul(2)
    for colour, axis in enumerate(first_axis):
        downs.append(links.copy(part.at[2, colour, low], full.at[1, colour, low], axis, -1))
    for colour, axis in enumerate(first_axis):
        up[colour].wait_recv()
        part[1, colour, low] += half[0, colour]
        ups.append(links.copy(part.at[1, colour, low], full.at[0, colour, low], axis, 1))
        down[colour].wait_recv()
        part[2, colour, high] += half[1, colour]
        downs.append(links.copy(part.at[2, colour, high], full.at[1, colour, high], axis, -1))
    matmul(3)
    for colour, axis in enumerate(first_axis):
        other = first_axis[1 - colour]
        arrive((ups[colour], downs[colour], ups[2 + colour], downs[2 + colour]))
        total = part[3, colour] + (full[0, colour] + full[1, colour])
        quarter[colour] = total.reshape(quarter.shape[1:])
        later.append(
            [
                links.copy(quarter.at[colour, place.of(other, step)], second.at[colour, step - 1], other, step)
                for step in (1, 2, 3)
            ]
        )
    for colour in range(2):
        arrive(later[colour])
        own[colour] = tree(quarter[colour, place[first_axis[1 - colour]]], second[colour])

    mine = own[...].reshape(-1, wide)
    h, m, l = split3(mine)
    left = jnp.concatenate([h, h, m, h, m, l], axis=0)

    def share(value, kind):
        for core in range(2):
            a, b, e = split3(value[:, core * 256 : core * 256 + 256])
            right = jnp.concatenate([a, b, a, e, b, a], axis=0)
            out = lax.dot_general(left, right, (((0,), (0,)), ((), ())), preferred_element_type=f32)
            for colour in range(2):
                parts[kind, core, colour] = out[:, colour * 128 : colour * 128 + 128].reshape(parts.shape[3:])

    grams, mixes = (
        Total(
            place, links, parts.at[kind], core_in.at[kind], v0.at[kind], r1.at[kind], v1.at[kind], r2.at[kind],
            v2.at[kind], r3.at[kind], v3.at[kind], w1.at[kind], w0.at[kind], totals.at[kind],
        )
        for kind in range(2)
    )
    gather, ring, relay = [], [], []

    def gather_first():
        for colour in range(2):
            axis, other = first_axis[colour], first_axis[1 - colour]
            s_buf[colour, place[axis], place[other]] = own[colour]
            here = s_buf.at[colour, place[axis], place[other]]
            gather.extend(links.copy(own.at[colour], here, other, step) for step in (1, 2, 3))

    def gather_ring():
        arrive(gather)
        for colour, axis in enumerate(first_axis):
            here = s_buf.at[colour, place[axis]]
            ring.extend((links.copy(here, here, axis, 1), links.copy(here, here, axis, -1)))

    def gather_relay():
        arrive(ring)
        for colour, axis in enumerate(first_axis):
            below = s_buf.at[colour, place.of(axis, -1), pl.ds(0, 2)]
            above = s_buf.at[colour, place.of(axis, 1), pl.ds(2, 2)]
            relay.extend((links.copy(below, below, axis, 1), links.copy(above, above, axis, -1)))

    size = 128
    rank = z_buf.shape[0]
    axes = (("y", "z"), ("z", "y"))
    across, firsts, fulls, lasts = [], [], [], []

    def turn_sketch():
        arrive(relay)
        for i in range(4):
            for colour in range(2):
                value = s_buf[colour, place.of(first_axis[colour], steps[i])].reshape(rows, rank).T
                start = (2 * i + colour) * rows
                high = value.astype(bf16)
                st_buf[0, :, start : start + rows] = high
                st_buf[1, :, start : start + rows] = (value - high.astype(f32)).astype(bf16)

    def multiply(b):
        block = g_buf[:, :, :, b * deep : b * deep + deep].reshape(8 * rows, deep)
        out = jnp.dot(st_buf[0], block, preferred_element_type=f32)
        out += jnp.dot(st_buf[1], block, preferred_element_type=f32)
        for i in range(deep // size):
            p = b * (deep // size) + i
            x_buf[p // 8, (p // 2) % 4, p % 2] = out[:, i * size : i * size + size].reshape(x_buf.shape[3:])
        if b == chunks - 1:
            for p in range(tiles, 32):
                x_buf[p // 8, (p // 2) % 4, p % 2] = jnp.zeros(x_buf.shape[3:], f32)
        for group in range(SIDE):
            if b == min(2 * group + 1, chunks - 1):
                across.append(links.copy(x_buf.at[group, :, 1 - c], x_in.at[group], "c", 1))

    def reduce_core(i):
        across[i].wait_recv()
        total = x_buf[i, :, c] + x_in[i]
        y_buf[0, i] = total[:, 0]
        y_buf[1, :, i] = total[:, 1]

    def reduce_ring():
        for colour in range(2):
            axis = axes[colour][0]
            far = place.of(axis, 2)
            firsts.append(links.copy(y_buf.at[colour, far, pl.ds(0, 2)], r_half.at[colour, 0], axis, 1))
            firsts.append(links.copy(y_buf.at[colour, far, pl.ds(2, 2)], r_half.at[colour, 1], axis, -1))

    def reduce_pass():
        for colour in range(2):
            axis = axes[colour][0]
            for side in range(2):
                firsts[2 * colour + side].wait_recv()
                to = place.of(axis, (1, -1)[side])
                y_buf[colour, to, 2 * side : 2 * side + 2] += r_half[colour, side]
                fulls.append(links.copy(y_buf.at[colour, to], r_full.at[colour, side], axis, (1, -1)[side]))

    def reduce_second():
        arrive(fulls)
        for colour in range(2):
            axis, other = axes[colour]
            p_buf[colour] = y_buf[colour, place[axis]] + (r_full[colour, 0] + r_full[colour, 1])
            lasts.extend(
                links.copy(p_buf.at[colour, place.of(other, step)], p_in.at[colour, step - 1], other, step)
                for step in (1, 2, 3)
            )

    def reduced():
        arrive(lasts)
        return jnp.concatenate(
            [tree(p_buf[colour, place[axes[colour][1]]], p_in[colour]) for colour in range(2)], axis=0
        )

    share(mine, 0)
    grams.core()
    gather_first()
    for out in o_loads:
        out.wait()
    share(o_buf[...].reshape(-1, wide), 1)
    grams.first()
    mixes.core()
    gather_ring()
    grams.second()
    grams.third()
    gather_relay()
    grams.back2()
    grams.back1()
    lax.fori_loop(1, 32, trade_start, 0)
    mc_buf[:, me] = m_buf[:, :, own_col]
    turn_sketch()
    multiply(0)
    grams.join()
    mixes.first()
    multiply(1)
    multiply(2)
    multiply(3)
    grams.end()
    mixes.second()
    multiply(4)
    multiply(5)
    mixes.third()
    multiply(6)

    for p in range(rank // size):
        z_buf[:, p * size : p * size + size] = totals[0, p // 2, p % 2].reshape(rank, size)

    def early():
        mixes.back2()
        for i in range(SIDE - 1):
            reduce_core(i)

    def start():
        mixes.back1()
        reduce_core(SIDE - 1)
        reduce_ring()

    def nothing():
        pass

    inverse_factor(
        z_buf,
        ticks=(early, start, nothing, mixes.join, reduce_pass, mixes.end, nothing, nothing),
    )

    def give(step, value, into, sems):
        to, source = lax.rem(me + step, 32), lax.rem(me + (32 - step), 32)
        return pltpu.make_async_remote_copy(
            src_ref=value.at[:, to],
            dst_ref=into.at[:, :, own_col],
            send_sem=tsend.at[sems, step],
            recv_sem=trecv.at[sems, step],
            device_id=device({**place.at, **plane_place(to)}),
            device_id_type=MESH,
        ), source

    gifts = ((turned, tin_ref), (made, pin_ref))

    def give_start(sems):
        def one(step, carry):
            out, source = give(step, *gifts[sems], sems)
            pl.when(me < tiles)(functools.partial(begin, out))
            return carry

        lax.fori_loop(1, 32, one, 0)

    def give_end(step, carry):
        for sems in range(2):
            out, source = give(step, *gifts[sems], sems)
            pl.when(me < tiles)(functools.partial(sent, out))
            pl.when(source < tiles)(functools.partial(came, out))
        return carry

    mixed = jnp.concatenate([totals[1, p // 2, p % 2].reshape(rank, size) for p in range(rank // size)], axis=1)
    half_rank = rank // 2
    for start_row in (0, half_rank):
        end_row = start_row + half_rank
        corr_buf[start_row:end_row] = jnp.dot(
            z_buf[start_row:end_row, 0:end_row], mixed[0:end_row], precision=HI, preferred_element_type=f32
        )
    reduce_second()
    lax.fori_loop(1, 32, trade_end, 0)
    corr = corr_buf[...]
    shape = turned.shape[1:]
    old = mc_buf[0].reshape(rank, size)
    turned[0] = jnp.dot(corr, old, precision=HI, preferred_element_type=f32).reshape(shape)
    old = mc_buf[1].reshape(rank, size)
    turned[1] = jnp.dot(corr * corr, old, precision=HI, preferred_element_type=f32).reshape(shape)
    give_start(0)
    made[0] = jnp.dot(z_buf[...], reduced(), precision=HI, preferred_element_type=f32).reshape(shape)
    give_start(1)

    @pl.when(me < tiles)
    def _():
        tin_ref[:, :, own_col] = turned[:, me]
        pin_ref[:, :, own_col] = made[:, me]

    lax.fori_loop(1, 32, give_end, 0)
    links.finish()


def call(grad, test, old, first, second):
    rows, cols = grad.shape
    rank = test.shape[1]
    deep = 512
    block, small = rows // 8, rows // 32
    strip = rank // SIDE
    bit = strip // SIDE
    own_rank, tiles = first.shape[0], cols // 128
    cut = rank // 2
    buf = lambda *shape: pltpu.VMEM(shape, f32)
    dma = lambda *shape: pltpu.SemaphoreType.DMA(shape)
    copies = 32 + 2 * 40 + 40
    return pl.pallas_call(
        functools.partial(kernel, tiles),
        out_shape=tuple(jax.ShapeDtypeStruct((n, own_rank, cols), f32) for n in (1, 2)),
        in_specs=[ANY, ANY, ANY, VMEM, VMEM],
        out_specs=(VMEM, VMEM),
        scratch_shapes=[
            pltpu.VMEM((4, 2, block, cols), bf16),
            pltpu.VMEM((cols // deep, deep, rank), jnp.int32),
            pltpu.VMEM((cols // deep, deep, rank), bf16),
            buf(4, 2, block, rank),
            buf(2, 2, block // 2, rank),
            buf(2, 2, block, rank),
            buf(2, SIDE, small, rank),
            buf(2, 3, small, rank),
            buf(2, small, rank),
            buf(2, small, rank),
            buf(2, 2, 2, SIDE, strip, 128),
            buf(2, 2, SIDE, strip, 128),
            buf(2, 2, SIDE, strip, 128),
            buf(2, 2, 3, strip, 128),
            buf(2, 2, SIDE, bit, 128),
            buf(2, 2, 3, bit, 128),
            buf(2, 2, bit, 128),
            buf(2, 2, 3, bit, 128),
            buf(2, 2, bit, 128),
            buf(2, 2, SIDE, bit, 128),
            buf(2, 2, SIDE, SIDE, bit, 128),
            buf(2, 2, 2, SIDE, SIDE, bit, 128),
            buf(2, SIDE, SIDE, small, rank),
            buf(2, own_rank, cols),
            buf(2, 32, own_rank, 128),
            buf(rank, rank),
            buf(rank, rank),
            buf(2, 32, own_rank, 128),
            buf(1, 32, own_rank, 128),
            pltpu.VMEM((2, rank, rows), bf16),
            buf(SIDE, SIDE, 2, 2, cut, 128),
            buf(SIDE, SIDE, 2, cut, 128),
            buf(2, SIDE, SIDE, cut, 128),
            buf(2, 2, 2, cut, 128),
            buf(2, 2, SIDE, cut, 128),
            buf(2, SIDE, cut, 128),
            buf(2, 3, cut, 128),
            dma(copies),
            dma(copies),
            dma(32),
            dma(32),
            dma(2, 32),
            dma(2, 32),
            dma(32),
        ],
        compiler_params=pltpu.CompilerParams(
            collective_id=0, has_side_effects=True, vmem_limit_bytes=67043328
        ),
    )(
        grad.reshape(2, SIDE, block, cols),
        test.reshape(cols // deep, deep, rank),
        old.reshape(2, SIDE, SIDE, small, rank),
        first,
        second,
    )


def finish_kernel(made_ref, turned_ref, projected_ref, first_ref, second_ref):
    projected = made_ref[0]
    projected_ref[...] = projected
    first_ref[...] = 0.9 * turned_ref[0] + 0.1 * projected
    second_ref[...] = 0.95 * turned_ref[1] + 0.05 * projected * projected


def local(gradients, test_matrix, old_basis, first_moment, second_moment):
    made, turned = call(gradients[0], test_matrix, old_basis, first_moment, second_moment)
    return pl.pallas_call(
        finish_kernel,
        out_shape=(jax.ShapeDtypeStruct(made.shape[1:], f32),) * 3,
        in_specs=[VMEM] * 2,
        out_specs=(VMEM,) * 3,
    )(made, turned)


def solution(mesh):
    moment = P(("dp", "row"), "col")
    in_specs = (P("dp", "row", "col"), P("col", None), P("row", None), moment, moment)
    return jax.shard_map(local, mesh=mesh, in_specs=in_specs, out_specs=(moment,) * 3, check_vma=False)
```

```python
import functools
import jax, jax.numpy as jnp
from jax import lax
from jax.experimental import pallas as pl
from jax.experimental.pallas import tpu as pltpu
from jax.sharding import PartitionSpec as P

HI = lax.Precision.HIGHEST
f32 = jnp.float32


def factor_diag(block, group, hooks):
    size = block.shape[0]
    tiles = size // 8
    z = [block[8 * b : 8 * b + 8, :] for b in range(tiles)]
    lane = lax.broadcasted_iota(jnp.int32, (8, size), 1)
    sub = lax.broadcasted_iota(jnp.int32, (8, size), 0)
    full = lambda v: jnp.broadcast_to(v, (8, size))
    for b in range(tiles):
        if b in hooks:
            hooks[b]()
        pivots = jnp.ones((8, size), f32)
        for r in range(0, 8, group):
            j = 8 * b + r
            piv = [[full(z[b][r + t : r + t + 1, j + s : j + s + 1]) for s in range(group)] for t in range(group)]
            inside = (lane >= j) & (lane < j + group)
            rows = [
                jnp.where(inside, (lane == j + t).astype(f32), full(z[b][r + t : r + t + 1, :])) for t in range(group)
            ]
            inv = []
            for t in range(group):
                pivots = jnp.where(sub == r + t, piv[t][t], pivots)
                inv.append(1.0 / piv[t][t])
                for u in range(t + 1, group):
                    m = piv[t][u] * inv[t]
                    for s in range(u, group):
                        piv[u][s] = piv[u][s] - piv[t][u] * piv[t][s] * inv[t]
                    rows[u] = rows[u] - m * rows[t]
            for i in range(b, tiles):
                cols = [full_col(z[i], j + t, size) for t in range(group)]
                acc = jnp.where(inside, (sub - r == lane - j).astype(f32) if i == b else 0.0, z[i])
                for t in range(group):
                    m = cols[t] * inv[t]
                    for u in range(t + 1, group):
                        cols[u] = cols[u] - m * piv[t][u]
                    if i == b:
                        m = jnp.where(sub > r + t, m, 0.0)
                    acc = acc - m * rows[t]
                z[i] = acc
        z[b] = z[b] * lax.rsqrt(pivots)
    out = jnp.concatenate(z, axis=0)
    i = lax.broadcasted_iota(jnp.int32, (size, size), 0)
    k = lax.broadcasted_iota(jnp.int32, (size, size), 1)
    return jnp.where(k <= i, out, 0.0)


def full_col(tile, j, size):
    return jnp.broadcast_to(tile[:, j : j + 1], (8, size))


def inverse_factor(z, ticks, group=8, size=128):
    n = z.shape[0]
    blocks = n // size
    for k in range(blocks):
        at = slice(k * size, k * size + size)
        inv = factor_diag(z[at, at], group, {tile: job for (block, tile), job in ticks.items() if block == k})
        z[at, :] = jnp.dot(inv, z[at, :], precision=HI, preferred_element_type=f32)
        z[at, at] = inv
        if k + 1 < blocks:
            below = slice(k * size + size, n)
            low = z[at, below]
            z[below, at] = jnp.zeros((n - below.start, size), f32)
            z[below, :] = z[below, :] - lax.dot_general(
                low, z[at, :], (((0,), (0,)), ((), ())), precision=HI, preferred_element_type=f32
            )
    row = lax.broadcasted_iota(jnp.int32, (n, n), 0) // size
    col = lax.broadcasted_iota(jnp.int32, (n, n), 1) // size
    z[...] = jnp.where(col <= row, z[...], 0.0)
MESH = pl.DeviceIdType.MESH
bf16 = jnp.bfloat16
SIDE = 4
VMEM = pl.BlockSpec(memory_space=pltpu.VMEM)
ANY = pl.BlockSpec(memory_space=pl.ANY)


def plane_place(p):
    return {"y": p // 8, "z": (p // 2) % 4, "c": p % 2}


def device(at):
    return (at["y"], at["z"] * 2 + at["c"], at["x"])


class Place:
    def __init__(self):
        row = lax.axis_index("row")
        self.at = {"x": lax.axis_index("col"), "y": lax.axis_index("dp"), "z": row // 2, "c": row % 2}
        self.rank = self.at["y"] * 8 + row
        self.near, self.devices = {}, {}
        for axis, here in self.at.items():
            size = 2 if axis == "c" else SIDE
            for step in range(size):
                there = lax.rem(here + step, size)
                self.near[axis, step] = there
                self.devices[axis, step] = device({**self.at, axis: there})

    def __getitem__(self, axis):
        return self.at[axis]

    def of(self, axis, step):
        return self.near[axis, step % SIDE]


class Copy:
    def __init__(self, links, src, dst, axis, step, number):
        self.links, self.src, self.dst, self.number = links, src, dst, number
        self.device = links.place.devices[axis, step % (2 if axis == "c" else SIDE)]

    def build(self):
        src, dst = (ref[0].at[ref[1]] if isinstance(ref, tuple) else ref for ref in (self.src, self.dst))
        return pltpu.make_async_remote_copy(
            src_ref=src,
            dst_ref=dst,
            send_sem=self.links.send.at[self.number],
            recv_sem=self.links.recv.at[self.number],
            device_id=self.device,
            device_id_type=MESH,
        )

    def wait_recv(self):
        self.build().wait_recv()

    def wait_send(self):
        self.build().wait_send()


class Links:
    def __init__(self, place, send, recv):
        self.place, self.send, self.recv, self.used, self.started = place, send, recv, 0, []

    def copy(self, src, dst, axis, step):
        out = Copy(self, src, dst, axis, step, self.used)
        self.used += 1
        self.started.append(out)
        out.build().start()
        return out

    def finish(self):
        for out in self.started:
            out.wait_send()


def begin(out):
    out.start()


def sent(out):
    out.wait_send()


def came(out):
    out.wait_recv()


def arrive(outs):
    for out in outs:
        out.wait_recv()


def tree(own, slots):
    return (own + slots[1]) + (slots[0] + slots[2])


def split3(value):
    high = value.astype(bf16)
    rest = value - high.astype(f32)
    mid = rest.astype(bf16)
    low = (rest - mid.astype(f32)).astype(bf16)
    return high, mid, low


class Total:
    orders = (("x", "z", "y"), ("y", "z", "x"))

    def __init__(self, place, links, parts, core_in, v0, r1, v1, r2, v2, r3, v3, w1, w0, out):
        self.place, self.links, self.parts, self.core_in, self.out = place, links, parts, core_in, out
        self.v0, self.r1, self.v1, self.r2, self.v2 = v0, r1, v1, r2, v2
        self.r3, self.v3, self.w1, self.w0 = r3, v3, w1, w0
        self.flying = []

    def steps(self):
        return (self.core, self.first, self.second, self.third, self.back2, self.back1, self.join, self.end)

    def core(self):
        self.flying = [self.links.copy(self.parts.at[1 - self.place["c"]], self.core_in, "c", 1)]

    def send(self, level, src, dst):
        arrivals = []
        for colour in range(2):
            axis = self.orders[colour][level]
            for step in (1, 2, 3):
                arrivals.append(self.links.copy(src(colour, axis, step), dst(colour, axis, step), axis, step))
        self.flying = arrivals

    def first(self):
        arrive(self.flying)
        self.v0[...] = self.parts[self.place["c"]] + self.core_in[...]
        self.send(
            0,
            lambda colour, axis, step: self.v0.at[colour, self.place.of(axis, step)],
            lambda colour, axis, step: self.r1.at[colour, step - 1],
        )

    def second(self):
        arrive(self.flying)
        for colour in range(2):
            mine = self.v0[colour, self.place[self.orders[colour][0]]]
            self.v1[colour] = tree(mine, self.r1[colour]).reshape(self.v1.shape[1:])
        self.send(
            1,
            lambda colour, axis, step: self.v1.at[colour, self.place.of(axis, step)],
            lambda colour, axis, step: self.r2.at[colour, step - 1],
        )

    def third(self):
        arrive(self.flying)
        for colour in range(2):
            self.v2[colour] = tree(self.v1[colour, self.place[self.orders[colour][1]]], self.r2[colour])
        self.send(
            2,
            lambda colour, axis, step: self.v2.at[colour],
            lambda colour, axis, step: self.r3.at[colour, step - 1],
        )

    def back2(self):
        arrive(self.flying)
        for colour in range(2):
            total = tree(self.v2[colour], self.r3[colour])
            self.v3[colour] = total
            self.w1[colour, self.place[self.orders[colour][1]]] = total
        self.send(
            1,
            lambda colour, axis, step: self.v3.at[colour],
            lambda colour, axis, step: self.w1.at[colour, self.place[axis]],
        )

    def back1(self):
        arrive(self.flying)
        for colour in range(2):
            self.w0[colour, self.place[self.orders[colour][0]]] = self.w1[colour]
        self.send(
            0,
            lambda colour, axis, step: self.w1.at[colour],
            lambda colour, axis, step: self.w0.at[colour, self.place[axis]],
        )

    def join(self):
        arrive(self.flying)
        c = self.place["c"]
        self.out[c] = self.w0[...]
        self.flying = [self.links.copy(self.w0, self.out.at[c], "c", 1)]

    def end(self):
        arrive(self.flying)


def kernel(
    tiles, g_hbm, t_hbm, o_hbm, m1_ref, m2_ref, pin_ref, tin_ref,
    g_buf, t_buf, t_low, part, half, full, quarter, second, own, o_buf,
    parts, core_in, v0, r1, v1, r2, v2, r3, v3, w1, w0, totals,
    s_buf, m_buf, mc_buf, z_buf, corr_buf, turned, made, st_buf,
    x_buf, x_in, y_buf, r_half, r_full, p_buf, p_in,
    send, recv, msend, mrecv, tsend, trecv, local_sem,
):
    place = Place()
    x, y, c, me = place["x"], place["y"], place["c"], place.rank
    links = Links(place, send, recv)
    first_axis = ("x", "y")

    barrier = pltpu.get_barrier_semaphore()

    def greet(step, carry):
        to = {**place.at, **plane_place(lax.rem(me + step, 32))}
        pl.semaphore_signal(barrier, inc=1, device_id=device(to), device_id_type=MESH)
        return carry

    loads = []

    def load(src, dst):
        out = pltpu.make_async_copy(src, dst, local_sem.at[len(loads)])
        out.start()
        loads.append(out)
        return out

    steps = (2, 1, -1, 0)
    chunks, deep, wide = t_buf.shape
    rows = g_buf.shape[2]
    g_loads, t_loads = {}, {}

    def load_g(i):
        g_loads[i] = [
            load(g_hbm.at[colour, place.of(first_axis[colour], steps[i])], g_buf.at[i, colour]) for colour in range(2)
        ]

    load_g(0)
    for k in range(chunks):
        t_loads[k] = load(t_hbm.at[k], t_buf.at[k])
    for i in (1, 2, 3):
        load_g(i)
    o_loads = [load(o_hbm.at[0, x, y], o_buf.at[0]), load(o_hbm.at[1, y, x], o_buf.at[1])]

    for step in (1, 2, 3):
        pl.semaphore_signal(barrier, inc=1, device_id=place.devices["x", step], device_id_type=MESH)
    lax.fori_loop(1, 32, greet, 0)

    def product(i, k):
        lhs = g_buf[i, :, :, pl.ds(pl.multiple_of(k * deep, deep), deep)].reshape(2 * rows, deep)
        return jnp.dot(lhs, t_low[k], preferred_element_type=f32).reshape(2, rows, wide)

    def matmul(i):
        for out in g_loads[i]:
            out.wait()
        if i == 0:
            for k in range(chunks):
                t_loads[k].wait()
                t_low[k] = t_buf[k].astype(f32).astype(bf16)
                part[i] = product(i, k) + (part[i] if k else 0.0)
        else:
            part[i] = product(i, 0)

            def more(k, carry):
                part[i] += product(i, k)
                return carry

            lax.fori_loop(1, chunks, more, 0)

    def trade(step):
        to = lax.rem(me + step, 32)
        col = pl.ds(pl.multiple_of(lax.rem(to, tiles) * 128, 128), 128)
        return pltpu.make_async_remote_copy(
            src_ref=m_buf.at[:, :, col],
            dst_ref=mc_buf.at[:, me],
            send_sem=msend.at[step],
            recv_sem=mrecv.at[step],
            device_id=device({**place.at, **plane_place(to)}),
            device_id_type=MESH,
        ), to

    def trade_start(step, carry):
        out, to = trade(step)
        pl.when(to < tiles)(functools.partial(begin, out))
        return carry

    def trade_end(step, carry):
        out, to = trade(step)
        pl.when(to < tiles)(functools.partial(sent, out))
        pl.when(me < tiles)(functools.partial(came, out))
        return carry

    own_col = pl.ds(pl.multiple_of(lax.rem(me, tiles) * 128, 128), 128)

    matmul(0)
    m_buf[0] = m1_ref[...]
    m_buf[1] = m2_ref[...]
    pl.semaphore_wait(barrier, 34)
    mid = rows // 2
    up, down, ups, downs, later = [], [], [], [], []
    for colour, axis in enumerate(first_axis):
        up.append(links.copy(part.at[0, colour, pl.ds(0, mid)], half.at[0, colour], axis, 1))
        down.append(links.copy(part.at[0, colour, pl.ds(mid, mid)], half.at[1, colour], axis, -1))
    matmul(1)
    low, high = pl.ds(0, mid), pl.ds(mid, mid)
    for colour, axis in enumerate(first_axis):
        ups.append(links.copy(part.at[1, colour, high], full.at[0, colour, high], axis, 1))
    matmul(2)
    for colour, axis in enumerate(first_axis):
        downs.append(links.copy(part.at[2, colour, low], full.at[1, colour, low], axis, -1))
    for colour, axis in enumerate(first_axis):
        up[colour].wait_recv()
        part[1, colour, low] += half[0, colour]
        ups.append(links.copy(part.at[1, colour, low], full.at[0, colour, low], axis, 1))
        down[colour].wait_recv()
        part[2, colour, high] += half[1, colour]
        downs.append(links.copy(part.at[2, colour, high], full.at[1, colour, high], axis, -1))
    matmul(3)
    for colour, axis in enumerate(first_axis):
        other = first_axis[1 - colour]
        arrive((ups[colour], downs[colour], ups[2 + colour], downs[2 + colour]))
        total = part[3, colour] + (full[0, colour] + full[1, colour])
        quarter[colour] = total.reshape(quarter.shape[1:])
        later.append(
            [
                links.copy(quarter.at[colour, place.of(other, step)], second.at[colour, step - 1], other, step)
                for step in (1, 2, 3)
            ]
        )
    for colour in range(2):
        arrive(later[colour])
        own[colour] = tree(quarter[colour, place[first_axis[1 - colour]]], second[colour])

    mine = own[...].reshape(-1, wide)
    h, m, l = split3(mine)
    left = jnp.concatenate([h, h, m, h, m, l], axis=0)

    def share(value, kind):
        for core in range(2):
            a, b, e = split3(value[:, core * 256 : core * 256 + 256])
            right = jnp.concatenate([a, b, a, e, b, a], axis=0)
            out = lax.dot_general(left, right, (((0,), (0,)), ((), ())), preferred_element_type=f32)
            for colour in range(2):
                parts[kind, core, colour] = out[:, colour * 128 : colour * 128 + 128].reshape(parts.shape[3:])

    grams, mixes = (
        Total(
            place, links, parts.at[kind], core_in.at[kind], v0.at[kind], r1.at[kind], v1.at[kind], r2.at[kind],
            v2.at[kind], r3.at[kind], v3.at[kind], w1.at[kind], w0.at[kind], totals.at[kind],
        )
        for kind in range(2)
    )
    gather, ring, relay = [], [], []

    def gather_first():
        for colour in range(2):
            axis, other = first_axis[colour], first_axis[1 - colour]
            s_buf[colour, place[axis], place[other]] = own[colour]
            here = s_buf.at[colour, place[axis], place[other]]
            gather.extend(links.copy(own.at[colour], here, other, step) for step in (1, 2, 3))

    def gather_ring():
        arrive(gather)
        for colour, axis in enumerate(first_axis):
            here = s_buf.at[colour, place[axis]]
            ring.extend((links.copy(here, here, axis, 1), links.copy(here, here, axis, -1)))

    def gather_relay():
        arrive(ring)
        for colour, axis in enumerate(first_axis):
            below = s_buf.at[colour, place.of(axis, -1), pl.ds(0, 2)]
            above = s_buf.at[colour, place.of(axis, 1), pl.ds(2, 2)]
            relay.extend((links.copy(below, below, axis, 1), links.copy(above, above, axis, -1)))

    size = 128
    rank = z_buf.shape[0]
    axes = (("y", "z"), ("z", "y"))
    across, firsts, fulls, lasts = [], [], [], []

    def turn_sketch(i):
        for colour in range(2):
            value = s_buf[colour, place.of(first_axis[colour], steps[i])].reshape(rows, rank).T
            start = (2 * i + colour) * rows
            high = value.astype(bf16)
            st_buf[0, :, start : start + rows] = high
            st_buf[1, :, start : start + rows] = (value - high.astype(f32)).astype(bf16)

    def multiply(b, low, high):
        block = g_buf[low:high, :, :, b * deep : b * deep + deep].reshape((high - low) * 2 * rows, deep)
        inner = slice(low * 2 * rows, high * 2 * rows)
        out = jnp.dot(st_buf[0, :, inner], block, preferred_element_type=f32)
        out += jnp.dot(st_buf[1, :, inner], block, preferred_element_type=f32)
        for i in range(deep // size):
            p = b * (deep // size) + i
            value = out[:, i * size : i * size + size].reshape(x_buf.shape[3:])
            if high < 4:
                value += x_buf[p // 8, (p // 2) % 4, p % 2]
            x_buf[p // 8, (p // 2) % 4, p % 2] = value
        if low > 0:
            return
        if b == chunks - 1:
            for p in range(tiles, 32):
                x_buf[p // 8, (p // 2) % 4, p % 2] = jnp.zeros(x_buf.shape[3:], f32)
        for group in range(SIDE):
            if b == min(2 * group + 1, chunks - 1):
                across.append(links.copy(x_buf.at[group, :, 1 - c], x_in.at[group], "c", 1))

    def reduce_core(i):
        across[i].wait_recv()
        total = x_buf[i, :, c] + x_in[i]
        y_buf[0, i] = total[:, 0]
        y_buf[1, :, i] = total[:, 1]

    half_cut = x_buf.shape[-2] // 2

    def reduce_ring(h):
        at = pl.ds(h * half_cut, half_cut)
        for colour in range(2):
            axis = axes[colour][0]
            far = place.of(axis, 2)
            for side in range(2):
                src = y_buf.at[colour, far, pl.ds(2 * side, 2), at]
                firsts.append(links.copy(src, r_half.at[colour, side, :, at], axis, (1, -1)[side]))

    def reduce_pass(h):
        at = pl.ds(h * half_cut, half_cut)
        for colour in range(2):
            axis = axes[colour][0]
            for side in range(2):
                firsts[4 * h + 2 * colour + side].wait_recv()
                to = place.of(axis, (1, -1)[side])
                y_buf[colour, to, 2 * side : 2 * side + 2, at] += r_half[colour, side, :, at]
                src = y_buf.at[colour, to, :, at]
                fulls.append(links.copy(src, r_full.at[colour, side, :, at], axis, (1, -1)[side]))

    def reduce_second(h):
        at = pl.ds(h * half_cut, half_cut)
        arrive(fulls[4 * h : 4 * h + 4])
        for colour in range(2):
            axis, other = axes[colour]
            p_buf[colour, :, at] = y_buf[colour, place[axis], :, at] + (
                r_full[colour, 0, :, at] + r_full[colour, 1, :, at]
            )
            lasts.extend(
                links.copy(
                    p_buf.at[colour, place.of(other, step), at], p_in.at[colour, step - 1, at], other, step
                )
                for step in (1, 2, 3)
            )

    def reduced():
        arrive(lasts)
        return jnp.concatenate(
            [tree(p_buf[colour, place[axes[colour][1]]], p_in[colour]) for colour in range(2)], axis=0
        )

    share(mine, 0)
    grams.core()
    gather_first()
    for out in o_loads:
        out.wait()
    share(o_buf[...].reshape(-1, wide), 1)
    grams.first()
    mixes.core()
    gather_ring()
    turn_sketch(3)
    for b in (0, 1, 2, 3):
        multiply(b, 3, 4)
    grams.second()
    mixes.first()
    for b in (4, 5, 6):
        multiply(b, 3, 4)
    grams.third()
    gather_relay()
    turn_sketch(1)
    turn_sketch(2)
    multiply(0, 1, 3)
    multiply(1, 1, 3)
    grams.back2()
    for b in (2, 3):
        multiply(b, 1, 3)
    mixes.second()
    for b in (4, 5):
        multiply(b, 1, 3)
    grams.back1()
    mixes.third()
    multiply(6, 1, 3)
    lax.fori_loop(1, 32, trade_start, 0)
    mc_buf[:, me] = m_buf[:, :, own_col]
    arrive(relay)
    turn_sketch(0)
    multiply(0, 0, 1)
    multiply(1, 0, 1)
    grams.join()
    mixes.back2()
    multiply(2, 0, 1)
    multiply(3, 0, 1)
    multiply(4, 0, 1)
    multiply(5, 0, 1)
    multiply(6, 0, 1)
    grams.end()

    for p in range(rank // size):
        z_buf[:, p * size : p * size + size] = totals[0, p // 2, p % 2].reshape(rank, size)

    def early():
        for i in range(SIDE - 1):
            reduce_core(i)
        mixes.back1()

    def start():
        reduce_core(SIDE - 1)
        reduce_ring(0)
        reduce_ring(1)

    inverse_factor(
        z_buf,
        ticks={
            (0, 8): early,
            (0, 12): start,
            (1, 4): mixes.join,
            (1, 12): lambda: reduce_pass(0),
            (2, 4): lambda: reduce_pass(1),
            (2, 12): mixes.end,
            (3, 8): lambda: reduce_second(0),
        },
    )

    def give(step, value, into, sems):
        to, source = lax.rem(me + step, 32), lax.rem(me + (32 - step), 32)
        return pltpu.make_async_remote_copy(
            src_ref=value.at[:, to],
            dst_ref=into.at[:, :, own_col],
            send_sem=tsend.at[sems, step],
            recv_sem=trecv.at[sems, step],
            device_id=device({**place.at, **plane_place(to)}),
            device_id_type=MESH,
        ), source

    gifts = ((turned, tin_ref), (made, pin_ref))

    def give_start(sems):
        def one(step, carry):
            out, source = give(step, *gifts[sems], sems)
            pl.when(me < tiles)(functools.partial(begin, out))
            return carry

        lax.fori_loop(1, 32, one, 0)

    def give_end(step, carry):
        for sems in range(2):
            out, source = give(step, *gifts[sems], sems)
            pl.when(me < tiles)(functools.partial(sent, out))
            pl.when(source < tiles)(functools.partial(came, out))
        return carry

    mixed = jnp.concatenate([totals[1, p // 2, p % 2].reshape(rank, size) for p in range(rank // size)], axis=1)
    half_rank = rank // 2
    for start_row in (0, half_rank):
        end_row = start_row + half_rank
        corr_buf[start_row:end_row] = jnp.dot(
            z_buf[start_row:end_row, 0:end_row], mixed[0:end_row], precision=HI, preferred_element_type=f32
        )
    reduce_second(1)
    lax.fori_loop(1, 32, trade_end, 0)
    corr = corr_buf[...]
    shape = turned.shape[1:]
    old = mc_buf[0].reshape(rank, size)
    turned[0] = jnp.dot(corr, old, precision=HI, preferred_element_type=f32).reshape(shape)
    old = mc_buf[1].reshape(rank, size)
    turned[1] = jnp.dot(corr * corr, old, precision=HI, preferred_element_type=f32).reshape(shape)
    give_start(0)
    made[0] = jnp.dot(z_buf[...], reduced(), precision=HI, preferred_element_type=f32).reshape(shape)
    give_start(1)

    @pl.when(me < tiles)
    def _():
        tin_ref[:, :, own_col] = turned[:, me]
        pin_ref[:, :, own_col] = made[:, me]

    lax.fori_loop(1, 32, give_end, 0)
    links.finish()


def call(grad, test, old, first, second):
    rows, cols = grad.shape
    rank = test.shape[1]
    deep = 512
    block, small = rows // 8, rows // 32
    strip = rank // SIDE
    bit = strip // SIDE
    own_rank, tiles = first.shape[0], cols // 128
    cut = rank // 2
    buf = lambda *shape: pltpu.VMEM(shape, f32)
    dma = lambda *shape: pltpu.SemaphoreType.DMA(shape)
    copies = 32 + 2 * 40 + 48
    return pl.pallas_call(
        functools.partial(kernel, tiles),
        out_shape=tuple(jax.ShapeDtypeStruct((n, own_rank, cols), f32) for n in (1, 2)),
        in_specs=[ANY, ANY, ANY, VMEM, VMEM],
        out_specs=(VMEM, VMEM),
        scratch_shapes=[
            pltpu.VMEM((4, 2, block, cols), bf16),
            pltpu.VMEM((cols // deep, deep, rank), jnp.int32),
            pltpu.VMEM((cols // deep, deep, rank), bf16),
            buf(4, 2, block, rank),
            buf(2, 2, block // 2, rank),
            buf(2, 2, block, rank),
            buf(2, SIDE, small, rank),
            buf(2, 3, small, rank),
            buf(2, small, rank),
            buf(2, small, rank),
            buf(2, 2, 2, SIDE, strip, 128),
            buf(2, 2, SIDE, strip, 128),
            buf(2, 2, SIDE, strip, 128),
            buf(2, 2, 3, strip, 128),
            buf(2, 2, SIDE, bit, 128),
            buf(2, 2, 3, bit, 128),
            buf(2, 2, bit, 128),
            buf(2, 2, 3, bit, 128),
            buf(2, 2, bit, 128),
            buf(2, 2, SIDE, bit, 128),
            buf(2, 2, SIDE, SIDE, bit, 128),
            buf(2, 2, 2, SIDE, SIDE, bit, 128),
            buf(2, SIDE, SIDE, small, rank),
            buf(2, own_rank, cols),
            buf(2, 32, own_rank, 128),
            buf(rank, rank),
            buf(rank, rank),
            buf(2, 32, own_rank, 128),
            buf(1, 32, own_rank, 128),
            pltpu.VMEM((2, rank, rows), bf16),
            buf(SIDE, SIDE, 2, 2, cut, 128),
            buf(SIDE, SIDE, 2, cut, 128),
            buf(2, SIDE, SIDE, cut, 128),
            buf(2, 2, 2, cut, 128),
            buf(2, 2, SIDE, cut, 128),
            buf(2, SIDE, cut, 128),
            buf(2, 3, cut, 128),
            dma(copies),
            dma(copies),
            dma(32),
            dma(32),
            dma(2, 32),
            dma(2, 32),
            dma(32),
        ],
        compiler_params=pltpu.CompilerParams(
            collective_id=0, has_side_effects=True, vmem_limit_bytes=67043328
        ),
    )(
        grad.reshape(2, SIDE, block, cols),
        test.reshape(cols // deep, deep, rank),
        old.reshape(2, SIDE, SIDE, small, rank),
        first,
        second,
    )


def finish_kernel(made_ref, turned_ref, projected_ref, first_ref, second_ref):
    projected = made_ref[0]
    projected_ref[...] = projected
    first_ref[...] = 0.9 * turned_ref[0] + 0.1 * projected
    second_ref[...] = 0.95 * turned_ref[1] + 0.05 * projected * projected


def local(gradients, test_matrix, old_basis, first_moment, second_moment):
    made, turned = call(gradients[0], test_matrix, old_basis, first_moment, second_moment)
    return pl.pallas_call(
        finish_kernel,
        out_shape=(jax.ShapeDtypeStruct(made.shape[1:], f32),) * 3,
        in_specs=[VMEM] * 2,
        out_specs=(VMEM,) * 3,
    )(made, turned)


def solution(mesh):
    moment = P(("dp", "row"), "col")
    in_specs = (P("dp", "row", "col"), P("col", None), P("row", None), moment, moment)
    return jax.shard_map(local, mesh=mesh, in_specs=in_specs, out_specs=(moment,) * 3, check_vma=False)
```
